32 devices in a mesh: fish: 4 (over y, core), curve: 8 (over z, x).
Axes of the slice: x: 2, y: 2, z: 4, core: 2. Of those that a mesh axis runs over, the one named last changes fastest.
Arguments:
- right_side: float32 [128, 128, 128], P('curve', 'fish'), may hold values from -36 to 36
- block_inverse: float32 [512, 512], replicated, may hold values from -1 to 1
- midline: float32 [7, 16, 256], P(None, 'fish'), may hold values from -2 to 10, as said below
- entry_fish: int32 [2048], P(('fish', 'curve')), may hold values from 0 to 3
- entry_seg: int32 [2048], P(('fish', 'curve')), may hold values from 0 to 240
- entry_dest: int32 [2048, 1], P(('fish', 'curve')), may hold values from 0 to 7; in each aligned block of 64 rows (0 to 63, 64 to 127, ...) at most 16 rows name the same one
- entry_block: int32 [2048], P(('fish', 'curve')), may hold values from 0 to 127
Outputs:
- pressure: float32 [128, 128, 128], P('curve', 'fish')
- residual: float32 [128, 128, 128], P('curve', 'fish')
- obstacle: bfloat16 [4, 128, 128, 128], P(None, 'curve', 'fish')
The draws below stay inside these ranges and needn't reach their ends.
Inputs may be any that keep to these rules, and one draw needn't show every extreme that they name: `midline`: positions lie within a few cells of the block that an entry names; half-widths are positive. `entry_dest`: within the 64 rows of one device no value appears more than 16 times, and in some devices' rows one value appears exactly 16 times.
All inputs are finite; a program needn't handle non-finite values.
Results may differ from the reference program's by a relative error of at most 0.004.
Values may be sent and summed in bfloat16 or wider, within the bound.
A program may use at most 64 MiB of HBM per device.

```python
import math
import jax
import jax.numpy as jnp
import numpy as np
from jax import lax

BE = 8
BLK = 512
BX_DEV = 2
BZ_DEV = 4
NY = 128
NPTS = 256
SEG = 16
FISH_GRP = 4
ENT_DEV = 64
ITERS = 2
CAP = 16
CZ = 32
NB = 128
X = 128
Z = 128
FISHES = 16
ENTRIES = 2048
N_FISH = 4
N_CURVE = 8


def draw_right_side(key, part):
    across = jnp.arange(X, dtype=jnp.float32) / X - 0.5
    depth = jnp.arange(Z, dtype=jnp.float32) / Z - 0.5
    scaling = (10.0 ** across)[:, None, None] * (3.0 ** depth)[None, :, None]
    base = jnp.clip(jax.random.normal(key, (X, Z, NY), jnp.float32), -6.0, 6.0)
    return base * scaling


def draw_block_inverse(key, part):
    subkeys = jax.random.split(jax.random.fold_in(key, 5), 2)
    spread = jax.random.uniform(subkeys[0], (BLK, BLK), jnp.float32, -1.0, 1.0) * (0.6 / math.sqrt(BLK))
    gains = jax.random.uniform(subkeys[1], (BLK,), jnp.float32, 0.8, 1.25)
    identity = jnp.eye(BLK, dtype=jnp.float32)
    return (identity * gains[None, :] + spread * (1.0 - identity)) / 7.0


def draw_midline(key, part):
    subkeys = jax.random.split(jax.random.fold_in(key, 7), 3)
    placed = jax.random.uniform(subkeys[0], (3, FISHES, NPTS), jnp.float32, -2.0, BE + 2.0)
    velocity = jnp.clip(jax.random.normal(subkeys[1], (3, FISHES, NPTS), jnp.float32), -2.0, 2.0)
    halfwidth = BE * jnp.exp(jax.random.uniform(subkeys[2], (1, FISHES, NPTS), jnp.float32, math.log(0.12), math.log(0.5)))
    return jnp.concatenate([placed, velocity, halfwidth], axis=0)


def touch_ends(drawn, rng, least, high):
    longest = drawn.shape.index(max(drawn.shape))
    spots = []
    for shift in (0, 1):
        where = [jax.random.randint(jax.random.fold_in(rng, axis), (), 0, length) for axis, length in enumerate(drawn.shape)]
        where[longest] = (where[longest] + shift) % drawn.shape[longest]
        spots.append(tuple(where))
    return drawn.at[spots[0]].set(least).at[spots[1]].set(high)


def shared_out(key, own, number, rows, amount, top, limit, skew):
    ranking = jax.random.permutation(key, amount)
    crowded, usual = load_shares(amount, rows * top, limit, skew, True), load_shares(amount, rows * top, limit, skew, False)
    places = jnp.arange(amount)

    def named(sizes, rotation):
        used = int((sizes > 0).sum())
        fixed = max(1, used // 4)
        passed = fixed + (places - fixed + rotation * (used - fixed)) % max(1, amount - fixed)
        return jnp.zeros((amount,), jnp.int32).at[ranking[jnp.where(places < fixed, places, passed)]].set(jnp.asarray(sizes, jnp.int32))

    sizes = jnp.where(number % 4 == 0, named(crowded, number // 4), named(usual, number - number // 4 - 1))
    mixed = jax.random.permutation(jax.random.fold_in(own, 3), amount)
    giver, sink = mixed[0:amount // 2 * 2:2], mixed[1:amount // 2 * 2:2]
    room = jnp.minimum(sizes[giver] - 1, limit - sizes[sink]) // 2
    room = jnp.where((giver == ranking[0]) | (sink == ranking[0]) | (sizes[sink] == 0), 0, jnp.maximum(room, 0))
    passed = jax.random.randint(jax.random.fold_in(own, 4), (amount // 2,), 0, 1 << 20) % (room + 1)
    sizes = sizes.at[giver].add(-passed).at[sink].add(passed)
    labels = jnp.searchsorted(jnp.cumsum(sizes), jnp.arange(rows * top), side="right").astype(jnp.int32)
    grid = labels.reshape(top, rows).T
    grid = grid[jax.random.permutation(jax.random.fold_in(own, 1), rows)]
    rotation = jax.random.randint(jax.random.fold_in(own, 2), (rows, 1), 0, top)
    return jnp.take_along_axis(grid, (jnp.arange(top)[None, :] + rotation) % top, axis=1)


def load_shares(number_of, total, limit, lean, full):
    portions = [(1 << 20) // math.isqrt(grade ** lean) + 1 for grade in range(1, number_of + 1)]
    largest = limit if full else min(limit, max(-(-total // number_of), total * portions[0] // sum(portions)))
    least = 1 if total - largest >= number_of - 1 else 0
    given, spare = [largest] + [least] * (number_of - 1), total - largest - least * (number_of - 1)
    while spare > 0:
        movable = [i for i in range(1, number_of) if given[i] < largest] or [i for i in range(1, number_of) if given[i] < limit]
        whole, left = sum([portions[i] for i in movable]), spare
        for i in movable:
            addition = min(limit - given[i], max(1, left * portions[i] // whole), spare)
            given[i] = given[i] + addition
            spare = spare - addition
    return np.array(given)


def setup_inputs(seed: int = 0) -> dict:
    seeds = jax.random.split(jax.random.key(seed), 8)
    right_side = draw_right_side(jax.random.fold_in(seeds[7], 71), 0)
    block_inverse = draw_block_inverse(jax.random.fold_in(seeds[7], 71), 0)
    midline = draw_midline(jax.random.fold_in(seeds[7], 71), 0)
    entry_fish = touch_ends(jax.random.randint(seeds[3], (ENTRIES,), 0, FISH_GRP), jax.random.fold_in(seeds[3], 1), 0, FISH_GRP - 1).astype(jnp.int32)
    entry_seg = touch_ends(jax.random.randint(seeds[4], (ENTRIES,), 0, NPTS - SEG + 1), jax.random.fold_in(seeds[4], 1), 0, NPTS - SEG).astype(jnp.int32)
    entry_dest_keys = jax.random.split(jax.random.fold_in(seeds[5], 1), ENTRIES // ENT_DEV)
    entry_dest_turns = jax.random.permutation(jax.random.fold_in(seeds[5], 3), ENTRIES // ENT_DEV)
    entry_dest = jax.vmap(lambda own, number: shared_out(jax.random.fold_in(seeds[5], 2), own, number, ENT_DEV, N_CURVE, 1, CAP, 2))(entry_dest_keys, entry_dest_turns).reshape((ENTRIES, 1))
    entry_block = touch_ends(jax.random.randint(seeds[6], (ENTRIES,), 0, NB), jax.random.fold_in(seeds[6], 1), 0, NB - 1).astype(jnp.int32)
    return {"right_side": right_side, "block_inverse": block_inverse, "midline": midline, "entry_fish": entry_fish, "entry_seg": entry_seg, "entry_dest": entry_dest, "entry_block": entry_block}


penalty = 4.0

def cell_coords(block_edge):
    cells = jnp.arange(block_edge * block_edge * block_edge, dtype=jnp.int32)
    xcoord = (cells // (block_edge * block_edge)).astype(jnp.float32) + 0.5
    zcoord = (cells // block_edge % block_edge).astype(jnp.float32) + 0.5
    ycoord = (cells % block_edge).astype(jnp.float32) + 0.5
    return (xcoord, ycoord, zcoord)

def lookup_points(table, which_fish, first_point, seg_len):
    flat_table = table.reshape(table.shape[0], -1)
    point_index = (which_fish * table.shape[2] + first_point)[:, None] + jnp.arange(seg_len, dtype=jnp.int32)[None, :]
    return jnp.take(flat_table, point_index.astype(jnp.int32), axis=1)

def build_payload(points, block_edge):
    xcoord, ycoord, zcoord = cell_coords(block_edge)
    count = points.shape[1]
    cells = xcoord.shape[0]

    def accumulate(index, carry):
        nearest, weight_sum, vel_x, vel_y, vel_z = carry
        column = lax.dynamic_slice_in_dim(points, index, 1, 2)[:, :, 0]
        delta_x = xcoord[None, :] - column[0][:, None]
        delta_y = ycoord[None, :] - column[1][:, None]
        delta_z = zcoord[None, :] - column[2][:, None]
        dist_sq = delta_x * delta_x + delta_y * delta_y + delta_z * delta_z
        signed = jnp.sqrt(dist_sq + 0.25) - column[6][:, None]
        weights = 1.0 / (1.0 + dist_sq)
        return (jnp.minimum(nearest, signed), weight_sum + weights, vel_x + weights * column[3][:, None], vel_y + weights * column[4][:, None], vel_z + weights * column[5][:, None])
    zeros = jnp.zeros((count, cells), jnp.float32)
    start = (jnp.full((count, cells), jnp.inf, jnp.float32), zeros, zeros, zeros, zeros)
    nearest, weight_sum, vel_x, vel_y, vel_z = lax.fori_loop(0, points.shape[2], accumulate, start)
    indicator = 0.5 - 0.5 * jnp.tanh(nearest)
    channels = [indicator, indicator * (vel_x / weight_sum), indicator * (vel_y / weight_sum), indicator * (vel_z / weight_sum)]
    return jnp.stack(channels, axis=1).astype(jnp.bfloat16)

def to_blocks(values, block_edge):
    size_x, size_z, size_y = values.shape
    shaped = values.reshape(size_x // block_edge, block_edge, size_z // block_edge, block_edge, size_y // block_edge, block_edge)
    return shaped.transpose(1, 3, 5, 0, 2, 4).reshape(block_edge ** 3, -1)

def to_field(blocks, block_edge, size_x, size_z, size_y):
    shaped = blocks.reshape(block_edge, block_edge, block_edge, size_x // block_edge, size_z // block_edge, size_y // block_edge)
    return shaped.transpose(3, 0, 4, 1, 5, 2).reshape(size_x, size_z, size_y)

def reference(right_side, block_inverse, midline, entry_fish, entry_seg, entry_dest, entry_block):
    table_groups = midline.reshape(7, N_FISH, FISH_GRP, NPTS).transpose(1, 0, 2, 3)
    per_group = N_CURVE * ENT_DEV

    def group_obstacle(inputs):
        table, which_fish, first_point, target, block_id = inputs

        def one_device(pieces):
            return build_payload(lookup_points(table, pieces[0], pieces[1], SEG), BE)
        payload = lax.map(one_device, (which_fish.reshape(N_CURVE, ENT_DEV), first_point.reshape(N_CURVE, ENT_DEV)))
        payload = payload.reshape(per_group, 4 * BLK).astype(jnp.float32)
        owner_block = (target * NB + block_id).astype(jnp.int32)
        summed = jax.ops.segment_sum(payload, owner_block, num_segments=N_CURVE * NB)
        owned = summed.astype(jnp.bfloat16).reshape(N_CURVE, NB, 4, BLK).transpose(2, 0, 3, 1)
        layout = owned.reshape(4, N_CURVE, BE, BE, BE, BX_DEV, BZ_DEV, NY // BE)
        layout = layout.transpose(0, 1, 5, 2, 6, 3, 7, 4)
        return layout.reshape(4, X, CZ, NY)
    groups = lax.map(group_obstacle, (table_groups, entry_fish.reshape(N_FISH, per_group), entry_seg.reshape(N_FISH, per_group), entry_dest[:, 0].reshape(N_FISH, per_group), entry_block.reshape(N_FISH, per_group)))
    obstacle = groups.transpose(1, 2, 0, 3, 4).reshape(4, X, Z, NY)
    diagonal = 6.0 + penalty * obstacle[0].astype(jnp.float32)
    source = right_side - (obstacle[1].astype(jnp.float32) + obstacle[2].astype(jnp.float32) + obstacle[3].astype(jnp.float32))

    def precondition(values):
        product = jnp.dot(block_inverse, to_blocks(values, BE), precision=lax.Precision.HIGHEST, preferred_element_type=jnp.float32)
        return to_field(product, BE, X, Z, NY)

    def operate(values):
        padded = jnp.pad(values, 1)
        beside = padded[2:, 1:-1, 1:-1] + padded[:-2, 1:-1, 1:-1]
        beside = beside + padded[1:-1, 2:, 1:-1] + padded[1:-1, :-2, 1:-1]
        beside = beside + padded[1:-1, 1:-1, 2:] + padded[1:-1, 1:-1, :-2]
        return diagonal * values - beside
    pressure = jnp.zeros_like(source)
    residual = source
    shadow = source
    direction = source
    rho_now = None
    for iteration in range(ITERS):
        precond_dir = precondition(direction)
        image_dir = operate(precond_dir)
        if iteration == 0:
            rho_now = jnp.sum(shadow * shadow)
        shadow_image = jnp.sum(shadow * image_dir)
        alpha_step = rho_now / shadow_image
        halfway = residual - alpha_step * image_dir
        precond_half = precondition(halfway)
        image_half = operate(precond_half)
        omega_step = jnp.sum(image_half * halfway) / jnp.sum(image_half * image_half)
        pressure = pressure + alpha_step * precond_dir + omega_step * precond_half
        residual = halfway - omega_step * image_half
        if iteration + 1 < ITERS:
            rho_next = jnp.sum(shadow * halfway) - omega_step * jnp.sum(shadow * image_half)
            beta_step = rho_next / rho_now * (alpha_step / omega_step)
            direction = residual + beta_step * (direction - omega_step * image_dir)
            rho_now = rho_next
    return (pressure, residual, obstacle)
```

```python
import functools
import jax
import jax.numpy as jnp
from jax import lax
from jax.experimental import pallas as pl
from jax.experimental.pallas import tpu as pltpu
from jax.sharding import PartitionSpec as P

BE = 8
SEG = 16
PENALTY = 4.0
F32 = jnp.float32
BF16 = jnp.bfloat16
MESH = pl.DeviceIdType.MESH


def nt_dot(a, b):
    return lax.dot_general(a, b, (((1,), (1,)), ((), ())), preferred_element_type=F32)


def nn_dot(a, b):
    return lax.dot_general(a, b, (((1,), (0,)), ((), ())), preferred_element_type=F32)


def split3(x):
    hi = x.astype(BF16)
    rest = x - hi.astype(F32)
    mid = rest.astype(BF16)
    low = (rest - mid.astype(F32)).astype(BF16)
    return hi, mid, low


def swap_bits(arrays, lane):
    arrays = list(arrays)
    lanes = lane.shape[-1]
    for step in (4, 2, 1):
        clear = (lane & step) == 0
        for a in range(8):
            if a & step:
                continue
            low, high = arrays[a], arrays[a | step]
            arrays[a] = jnp.where(clear, low, pltpu.roll(high, step, axis=1))
            arrays[a | step] = jnp.where(clear, pltpu.roll(low, lanes - step, axis=1), high)
    return arrays


def kernel(
    nf, nc, cap, npts,
    rs_ref, inv_ref, table_ref, meta_ref,
    press_ref, resid_ref, obst_ref,
    mh, ml, gath, shifted, pt, dyz, ob, src, diag,
    y1, v1, m1, w1, n1, u1, m2, w2,
    xsend, zsend, xlow, xhigh, zlow, zhigh, rsend, rfish, rcurve,
    gsend_sem, grecv_sem, hsend_sem, hrecv_sem, fsend_sem, frecv_sem, csend_sem, crecv_sem,
):
    mf = lax.axis_index("fish")
    mc = lax.axis_index("curve")
    cells, lanes = src.shape
    slab = BE * BE
    bx_n = rs_ref.shape[0] // BE
    bz_n = rs_ref.shape[1] // BE
    group = bx_n * bz_n

    barrier = pltpu.get_barrier_semaphore()

    def greet_fish(k, _):
        pl.semaphore_signal(
            barrier, inc=1, device_id=(lax.rem(mf + k, nf), mc), device_id_type=MESH
        )
        return 0

    def greet_curve(k, _):
        pl.semaphore_signal(
            barrier, inc=1, device_id=(mf, lax.rem(mc + k, nc)), device_id_type=MESH
        )
        return 0

    xlow[...] = jnp.zeros_like(xlow)
    xhigh[...] = jnp.zeros_like(xhigh)
    zlow[...] = jnp.zeros_like(zlow)
    zhigh[...] = jnp.zeros_like(zhigh)
    lax.fori_loop(1, nf, greet_fish, 0)
    lax.fori_loop(1, nc, greet_curve, 0)

    def peers(axis, src_at, dst, send_sem, recv_sem):
        count = nf if axis == "fish" else nc
        me = mf if axis == "fish" else mc

        def copy(k, slot, target):
            device = (target, mc) if axis == "fish" else (mf, target)
            return pltpu.make_async_remote_copy(
                src_ref=src_at,
                dst_ref=dst.at[slot],
                send_sem=send_sem.at[k],
                recv_sem=recv_sem.at[k],
                device_id=device,
                device_id_type=MESH,
            )

        def start():
            def body(k, _):
                copy(k, me, lax.rem(me + k, count)).start()
                return 0

            lax.fori_loop(1, count, body, 0)

        def finish():
            def body(k, _):
                origin = lax.rem(me + count - k, count)
                copy(k, origin, origin).wait()
                return 0

            lax.fori_loop(1, count, body, 0)

        return start, finish

    pl.semaphore_wait(barrier, nf - 1 + nc - 1)
    gstart, gfinish = peers("curve", meta_ref, gath, gsend_sem, grecv_sem)
    gath[mc] = meta_ref[...]
    gstart()

    lane8 = lax.broadcasted_iota(jnp.int32, (BE, lanes), 1)
    lane64 = lax.broadcasted_iota(jnp.int32, (slab, lanes), 1)
    lane32 = lax.broadcasted_iota(jnp.int32, (slab // 2, lanes), 1)
    sub8 = lax.broadcasted_iota(jnp.int32, (BE, lanes), 0)

    table = table_ref[...]
    width = table.shape[1]
    for m in range(SEG):
        turned = table if m == 0 else pltpu.roll(table, width - m, axis=1)
        shifted[m * 8 : m * 8 + 8, :] = turned

    whole = inv_ref[...]
    hi = whole.astype(BF16)
    mh[...] = hi
    ml[...] = (whole - hi.astype(F32)).astype(BF16)

    def field_to_rows(read, out_ref):
        parts = []
        for g in range(group):
            bx, bz = g // bz_n, g % bz_n
            parts.append(read(bx, bz).reshape(slab, lanes))
        for j, rows in enumerate(swap_bits(parts, lane64)):
            out_ref[pl.ds(j, slab, stride=BE), :] = rows

    def rows_to_field(read_j, write):
        parts = swap_bits([read_j(j) for j in range(BE)], lane64)
        for bx in range(bx_n):
            for i in range(BE):
                plane = jnp.concatenate(
                    [parts[bx * bz_n + bz][i * BE : (i + 1) * BE, :] for bz in range(bz_n)], axis=0
                )
                write(bx * BE + i, plane)

    field_to_rows(
        lambda bx, bz: rs_ref[bx * BE : (bx + 1) * BE, bz * BE : (bz + 1) * BE, :], src
    )

    gfinish()

    col = lax.broadcasted_iota(jnp.int32, (lanes, lanes), 1)
    row = lax.broadcasted_iota(jnp.int32, (lanes, lanes), 0)
    earlier = jnp.where(row < col, 1.0, 0.0).astype(BF16)
    mine = gath[:, 2, :] == mc.astype(F32)
    rank = nn_dot(jnp.where(mine, 1.0, 0.0).astype(BF16), earlier)
    origin = lax.broadcasted_iota(jnp.int32, (nc, lanes), 0).astype(F32)
    slot = jnp.where(mine, origin * cap + rank, -1.0)
    rowf = row.astype(F32)
    picked = jnp.zeros((8, lanes), F32)
    for c in range(nc):
        hot = jnp.where(rowf == slot[c : c + 1, :], 1.0, 0.0).astype(BF16)
        picked = picked + nt_dot(gath[c].astype(BF16), hot)
    index = picked[0:1, :] * npts + picked[1:2, :]
    place = picked[3:4, :] - 1.0
    block_hot = jnp.where(rowf == place, 1.0, 0.0).astype(BF16)
    point_hot = jnp.where(
        lax.broadcasted_iota(jnp.int32, (width, lanes), 0).astype(F32) == index, 1.0, 0.0
    ).astype(BF16)
    hi, mid, low = split3(shifted[...])
    pt[...] = (nn_dot(hi, point_hot) + nn_dot(mid, point_hot)) + nn_dot(low, point_hot)

    cell = lax.broadcasted_iota(jnp.int32, (slab, lanes), 0)
    zc = (cell // BE).astype(F32) + 0.5
    yc = (cell % BE).astype(F32) + 0.5
    for m in range(SEG):
        dy = yc - pt[m * 8 + 1 : m * 8 + 2, :]
        dz = zc - pt[m * 8 + 2 : m * 8 + 3, :]
        dyz[m] = dy * dy + dz * dz

    half = slab // 2

    def build(i, _):
        xc = i.astype(F32) + 0.5
        for h in range(2):
            lo_row = h * half
            near = ws = vx = vy = vz = None
            for m in range(SEG):
                dx = xc - pt[m * 8 : m * 8 + 1, :]
                d = dyz[m, lo_row : lo_row + half, :] + dx * dx
                e = d + 0.25
                signed = e * lax.rsqrt(e) - pt[m * 8 + 6 : m * 8 + 7, :]
                a = 1.0 / (1.0 + d)
                ax = a * pt[m * 8 + 3 : m * 8 + 4, :]
                ay = a * pt[m * 8 + 4 : m * 8 + 5, :]
                az = a * pt[m * 8 + 5 : m * 8 + 6, :]
                if m == 0:
                    near, ws, vx, vy, vz = signed, a, ax, ay, az
                else:
                    near = jnp.minimum(near, signed)
                    ws, vx, vy, vz = ws + a, vx + ax, vy + ay, vz + az
            ind = 0.5 - 0.5 * jnp.tanh(near)
            scale = 1.0 / ws
            pay = jnp.concatenate(
                [ind, ind * (vx * scale), ind * (vy * scale), ind * (vz * scale)], axis=0
            ).astype(BF16)
            summed = nt_dot(pay, block_hot).astype(BF16).astype(F32)
            base = pl.multiple_of(i * slab + lo_row, half)
            for c in range(4):
                ob[c, pl.ds(base, half), :] = summed[c * half : (c + 1) * half, :]
        return 0

    lax.fori_loop(0, BE, build, 0)
    diag[...] = 6.0 + PENALTY * ob[0]
    src[...] = src[...] - ((ob[1] + ob[2]) + ob[3])

    def precondition(value, out_ref):
        vh = value.astype(BF16)
        vl = (value - vh.astype(F32)).astype(BF16)
        wide = nn_dot(mh[...], jnp.concatenate([vh, vl], axis=1))
        out_ref[...] = (wide[:, :lanes] + wide[:, lanes:]) + nn_dot(ml[...], vh)

    bz8 = lane8 % bz_n
    bx8 = (lane8 // bz_n) % bx_n
    bx64 = (lane64 // bz_n) % bx_n
    bx32 = (lane32 // bz_n) % bx_n

    def turn(x, shift):
        shift = shift % lanes
        return x if shift == 0 else pltpu.roll(x, shift, axis=1)

    def halo(turn_no):
        def copy(buf, dst, k, device):
            return pltpu.make_async_remote_copy(
                src_ref=buf,
                dst_ref=dst.at[turn_no],
                send_sem=hsend_sem.at[turn_no, k],
                recv_sem=hrecv_sem.at[turn_no, k],
                device_id=device,
                device_id_type=MESH,
            )

        down_c = copy(xsend.at[turn_no, 0], xhigh, 0, (mf, lax.max(mc - 1, 0)))
        up_c = copy(xsend.at[turn_no, 1], xlow, 1, (mf, lax.min(mc + 1, nc - 1)))
        down_f = copy(zsend.at[turn_no, 0], zhigh, 2, (lax.max(mf - 1, 0), mc))
        up_f = copy(zsend.at[turn_no, 1], zlow, 3, (lax.min(mf + 1, nf - 1), mc))
        return down_c, up_c, down_f, up_f

    def operate(v_ref, out_ref, turn_no):
        v0 = v_ref[0:slab, :]
        v7 = v_ref[cells - slab : cells, :]
        xsend[turn_no, 0] = jnp.where(bx32 == 0, v0[:half], turn(v0[half:], bz_n))
        xsend[turn_no, 1] = jnp.where(bx32 == 0, turn(v7[:half], -bz_n), v7[half:])
        for t in range(2):
            lowp = highp = None
            for a in range(bz_n):
                start = (t * bz_n + a) * slab
                lo = turn(v_ref[start : start + BE, :], a)
                hg = turn(v_ref[start + slab - BE : start + slab, :], a - (bz_n - 1))
                lowp = lo if a == 0 else jnp.where(bz8 == a, lo, lowp)
                highp = hg if a == 0 else jnp.where(bz8 == a, hg, highp)
            zsend[turn_no, 0, t * BE : (t + 1) * BE, :] = lowp
            zsend[turn_no, 1, t * BE : (t + 1) * BE, :] = highp
        down_c, up_c, down_f, up_f = halo(turn_no)
        has = (mc > 0, mc < nc - 1, mf > 0, mf < nf - 1)
        for cond, cp in zip(has, (down_c, up_c, down_f, up_f)):
            pl.when(cond)(cp.start)

        for i in range(BE):
            v = v_ref[i * slab : (i + 1) * slab, :]
            if i > 0:
                beside = v_ref[(i - 1) * slab : i * slab, :]
            else:
                beside = jnp.where(bx64 > 0, turn(v7, bz_n), 0.0)
            if i < BE - 1:
                beside = beside + v_ref[(i + 1) * slab : (i + 2) * slab, :]
            else:
                beside = beside + jnp.where(bx64 < bx_n - 1, turn(v0, -bz_n), 0.0)
            rows = []
            for k in range(BE):
                t = v[k * BE : (k + 1) * BE, :]
                if k > 0:
                    s = v[(k - 1) * BE : k * BE, :]
                else:
                    s = jnp.where(bz8 > 0, turn(v[slab - BE :, :], 1), 0.0)
                if k < BE - 1:
                    s = s + v[(k + 1) * BE : (k + 2) * BE, :]
                else:
                    s = s + jnp.where(bz8 < bz_n - 1, turn(v[:BE, :], -1), 0.0)
                down = pltpu.roll(t, 1, axis=0)
                edge = jnp.where(lane8 < group, 0.0, turn(down, group))
                s = s + jnp.where(sub8 == 0, edge, down)
                up = pltpu.roll(t, BE - 1, axis=0)
                edge = jnp.where(lane8 >= lanes - group, 0.0, turn(up, -group))
                s = s + jnp.where(sub8 == BE - 1, edge, up)
                rows.append(s)
            beside = beside + jnp.concatenate(rows, axis=0)
            out_ref[i * slab : (i + 1) * slab, :] = (
                diag[i * slab : (i + 1) * slab, :] * v - beside
            )

        for cond, cp in zip((has[1], has[0], has[3], has[2]), (down_c, up_c, down_f, up_f)):
            pl.when(cond)(cp.wait_recv)
        for cond, cp in zip(has, (down_c, up_c, down_f, up_f)):
            pl.when(cond)(cp.wait_send)

        got = xhigh[turn_no]
        for h, part in enumerate((turn(got, bz_n), got)):
            a = cells - slab + h * half
            out_ref[a : a + half, :] = out_ref[a : a + half, :] - jnp.where(
                bx32 == bx_n - 1, part, 0.0
            )
        got = xlow[turn_no]
        for h, part in enumerate((got, turn(got, -bz_n))):
            a = h * half
            out_ref[a : a + half, :] = out_ref[a : a + half, :] - jnp.where(bx32 == 0, part, 0.0)
        for t in range(2):
            gl = zlow[turn_no, t * BE : (t + 1) * BE, :]
            gh = zhigh[turn_no, t * BE : (t + 1) * BE, :]
            for a in range(bz_n):
                start = (t * bz_n + a) * slab
                out_ref[start : start + BE, :] = out_ref[start : start + BE, :] - jnp.where(
                    bz8 == 0, turn(gl, -a), 0.0
                )
                b = start + slab - BE
                out_ref[b : b + BE, :] = out_ref[b : b + BE, :] - jnp.where(
                    bz8 == bz_n - 1, turn(gh, bz_n - 1 - a), 0.0
                )

    def pack(pairs):
        rows = [jnp.sum(a * b, axis=0, keepdims=True) for a, b in pairs]
        rows += [jnp.zeros((1, lanes), F32)] * (8 - len(rows))
        return jnp.concatenate(rows, axis=0)

    def reduction(no):
        fstart, ffinish = peers(
            "fish", rsend.at[no, 0], rfish.at[no], fsend_sem.at[no], frecv_sem.at[no]
        )
        cstart, cfinish = peers(
            "curve", rsend.at[no, 1], rcurve.at[no], csend_sem.at[no], crecv_sem.at[no]
        )

        def first(tile):
            rsend[no, 0] = tile
            rfish[no, mf] = tile
            fstart()

        def second():
            ffinish()
            tile = jnp.sum(rfish[no], axis=0)
            rsend[no, 1] = tile
            rcurve[no, mc] = tile
            cstart()

        def last():
            cfinish()
            tile = jnp.sum(rcurve[no], axis=0)
            total = jnp.sum(tile, axis=1, keepdims=True)
            return [total[r : r + 1, :] for r in range(8)]

        return first, second, last

    precondition(src[...], y1)
    operate(y1, v1, 0)
    precondition(v1[...], m1)
    operate(m1, w1, 1)
    first, second, last = reduction(0)
    r, v, w = src[...], v1[...], w1[...]
    first(pack([(r, r), (r, v), (v, v), (v, w), (w, w), (r, w)]))
    precondition(w1[...], n1)
    second()
    operate(n1, u1, 2)
    for c in range(4):
        def write(x, plane, c=c):
            obst_ref[c, x] = plane.astype(BF16)

        rows_to_field(lambda j, c=c: ob[c, pl.ds(j, slab, stride=BE), :], write)
    rr, rv, vv, vw, ww, rw, _, _ = last()
    alpha = rr / rv
    ts = (rv - alpha * vv) - alpha * (rw - alpha * vw)
    tt = (vv - alpha * vw) - alpha * (vw - alpha * ww)
    omega = ts / tt
    rho2 = (rr - alpha * rv) - omega * (rv - alpha * rw)
    beta = rho2 / rr * (alpha / omega)

    both, prod = alpha + omega, alpha * omega
    r = src[...]
    v, w = v1[...], w1[...]
    r2 = r - both * v + prod * w
    q = v - both * w + prod * u1[...]
    v2 = q + beta * (v - omega * w)
    mr2 = y1[...] - both * m1[...] + prod * n1[...]
    y2 = mr2 + beta * (y1[...] - omega * m1[...])
    n1[...] = alpha * y1[...] + omega * (y1[...] - alpha * m1[...])
    diag_keep = diag
    y1[...] = y2
    m1[...] = mr2
    w1[...] = r2
    u1[...] = q
    v1[...] = v2
    precondition(v2, m2)
    operate(m2, w2, 3)
    r2, q, v2, w = w1[...], u1[...], v1[...], w2[...]
    first, second, last = reduction(1)
    first(
        pack([(src[...], v2), (q, r2), (q, v2), (w, r2), (w, v2), (q, q), (q, w), (w, w)])
    )
    second()
    sv, qr, qv, wr, wv, qq, qw, ww = last()
    alpha2 = rho2 / sv
    ts = (qr - alpha2 * qv) - alpha2 * (wr - alpha2 * wv)
    tt = (qq - alpha2 * qw) - alpha2 * (qw - alpha2 * ww)
    omega2 = ts / tt
    src[...] = n1[...] + alpha2 * y1[...] + omega2 * (m1[...] - alpha2 * m2[...])
    diag_keep[...] = (w1[...] - alpha2 * v1[...]) - omega2 * (u1[...] - alpha2 * w2[...])

    def write_press(x, plane):
        press_ref[x] = plane

    def write_resid(x, plane):
        resid_ref[x] = plane

    rows_to_field(lambda j: src[pl.ds(j, slab, stride=BE), :], write_press)
    rows_to_field(lambda j: diag_keep[pl.ds(j, slab, stride=BE), :], write_resid)


def local(right_side, block_inverse, midline, entry_fish, entry_seg, entry_dest, entry_block):
    nf, nc = lax.axis_size("fish"), lax.axis_size("curve")
    count = entry_fish.shape[0]
    cap = max(2, 2 * count // nc)
    cx, cz, ny = right_side.shape
    lanes = (cx // BE) * (cz // BE) * (ny // BE)
    cells = BE**3
    slab = BE * BE
    rows, fishes, npts = midline.shape
    nyb = ny // BE
    group = (cx // BE) * (cz // BE)
    place = entry_block % nyb * group + entry_block // nyb
    meta = jnp.stack([entry_fish, entry_seg, entry_dest[:, 0], place + 1]).astype(F32)
    meta = jnp.pad(meta, ((0, 4), (0, lanes - count)), constant_values=-1.0)
    table = jnp.pad(midline.reshape(rows, fishes * npts), ((0, 8 - rows), (0, 0)))
    width = fishes * npts
    vmem = pl.BlockSpec(memory_space=pltpu.VMEM)
    big = pltpu.VMEM((cells, lanes), F32)
    dma = pltpu.SemaphoreType.DMA
    return pl.pallas_call(
        functools.partial(kernel, nf, nc, cap, npts),
        out_shape=(
            jax.ShapeDtypeStruct((cx, cz, ny), F32),
            jax.ShapeDtypeStruct((cx, cz, ny), F32),
            jax.ShapeDtypeStruct((4, cx, cz, ny), BF16),
        ),
        in_specs=[vmem] * 4,
        out_specs=(vmem, vmem, vmem),
        scratch_shapes=[
            pltpu.VMEM((cells, cells), BF16),
            pltpu.VMEM((cells, cells), BF16),
            pltpu.VMEM((nc, 8, lanes), F32),
            pltpu.VMEM((SEG * 8, width), F32),
            pltpu.VMEM((SEG * 8, lanes), F32),
            pltpu.VMEM((SEG, slab, lanes), F32),
            pltpu.VMEM((4, cells, lanes), F32),
        ]
        + [big] * 10
        + [
            pltpu.VMEM((4, 2, slab // 2, lanes), F32),
            pltpu.VMEM((4, 2, 2 * BE, lanes), F32),
            pltpu.VMEM((4, slab // 2, lanes), F32),
            pltpu.VMEM((4, slab // 2, lanes), F32),
            pltpu.VMEM((4, 2 * BE, lanes), F32),
            pltpu.VMEM((4, 2 * BE, lanes), F32),
            pltpu.VMEM((2, 2, 8, lanes), F32),
            pltpu.VMEM((2, nf, 8, lanes), F32),
            pltpu.VMEM((2, nc, 8, lanes), F32),
            dma((nc,)),
            dma((nc,)),
            dma((4, 4)),
            dma((4, 4)),
            dma((2, nf)),
            dma((2, nf)),
            dma((2, nc)),
            dma((2, nc)),
        ],
        compiler_params=pltpu.CompilerParams(collective_id=0, has_side_effects=True),
    )(right_side, block_inverse, table, meta)


def solution(mesh):
    return jax.shard_map(
        local,
        mesh=mesh,
        in_specs=(
            P("curve", "fish", None),
            P(),
            P(None, "fish", None),
            P(("fish", "curve")),
            P(("fish", "curve")),
            P(("fish", "curve"), None),
            P(("fish", "curve")),
        ),
        out_specs=(
            P("curve", "fish", None),
            P("curve", "fish", None),
            P(None, "curve", "fish", None),
        ),
        check_vma=False,
    )
```

```python
import functools
import jax
import jax.numpy as jnp
from jax import lax
from jax.experimental import pallas as pl
from jax.experimental.pallas import tpu as pltpu
from jax.sharding import PartitionSpec as P

BE = 8
SEG = 16
PENALTY = 4.0
F32 = jnp.float32
BF16 = jnp.bfloat16
MESH = pl.DeviceIdType.MESH


def nt_dot(a, b):
    return lax.dot_general(a, b, (((1,), (1,)), ((), ())), preferred_element_type=F32)


def nn_dot(a, b):
    return lax.dot_general(a, b, (((1,), (0,)), ((), ())), preferred_element_type=F32)


def split3(x):
    hi = x.astype(BF16)
    rest = x - hi.astype(F32)
    mid = rest.astype(BF16)
    low = (rest - mid.astype(F32)).astype(BF16)
    return hi, mid, low


def swap_bits(arrays, lane):
    arrays = list(arrays)
    lanes = lane.shape[-1]
    for step in (4, 2, 1):
        clear = (lane & step) == 0
        for a in range(8):
            if a & step:
                continue
            low, high = arrays[a], arrays[a | step]
            arrays[a] = jnp.where(clear, low, pltpu.roll(high, step, axis=1))
            arrays[a | step] = jnp.where(clear, pltpu.roll(low, lanes - step, axis=1), high)
    return arrays


def kernel(
    nf, nc, cap, npts,
    rs_ref, inv_ref, mid_ref, fish_ref, seg_ref, dest_ref, block_ref,
    press_ref, resid_ref, obst_ref,
    mh, ml, rhs, meta_ref, tab, gath, shifted, pt, dyz, ob, src, diag,
    y1, v1, m1, w1, n1, u1, m2, w2,
    xsend, zsend, xlow, xhigh, zlow, zhigh, rsend, rfish, rcurve,
    gsend_sem, grecv_sem, hsend_sem, hrecv_sem, fsend_sem, frecv_sem, csend_sem, crecv_sem,
):
    mf = lax.axis_index("fish")
    mc = lax.axis_index("curve")
    cells, lanes = src.shape
    slab = BE * BE
    bx_n = rs_ref.shape[0] // BE
    bz_n = rs_ref.shape[1] // BE
    group = bx_n * bz_n

    barrier = pltpu.get_barrier_semaphore()

    def greet_fish(k, _):
        pl.semaphore_signal(
            barrier, inc=1, device_id=(lax.rem(mf + k, nf), mc), device_id_type=MESH
        )
        return 0

    def greet_curve(k, _):
        pl.semaphore_signal(
            barrier, inc=1, device_id=(mf, lax.rem(mc + k, nc)), device_id_type=MESH
        )
        return 0

    nyb = rs_ref.shape[2] // BE
    count = fish_ref.shape[1]
    meta_ref[...] = jnp.full_like(meta_ref, -1.0)
    block = block_ref[...]
    place_in = block % nyb * group + block // nyb + 1
    for r, column in enumerate((fish_ref[...], seg_ref[...], dest_ref[...], place_in)):
        meta_ref[r : r + 1, 0:count] = column.astype(F32)
    xlow[...] = jnp.zeros_like(xlow)
    xhigh[...] = jnp.zeros_like(xhigh)
    zlow[...] = jnp.zeros_like(zlow)
    zhigh[...] = jnp.zeros_like(zhigh)
    lax.fori_loop(1, nf, greet_fish, 0)
    lax.fori_loop(1, nc, greet_curve, 0)

    def peers(axis, src_at, dst, send_sem, recv_sem):
        count = nf if axis == "fish" else nc
        me = mf if axis == "fish" else mc

        def copy(k, slot, target):
            device = (target, mc) if axis == "fish" else (mf, target)
            return pltpu.make_async_remote_copy(
                src_ref=src_at,
                dst_ref=dst.at[slot],
                send_sem=send_sem.at[k],
                recv_sem=recv_sem.at[k],
                device_id=device,
                device_id_type=MESH,
            )

        def start():
            def body(k, _):
                copy(k, me, lax.rem(me + k, count)).start()
                return 0

            lax.fori_loop(1, count, body, 0)

        def finish():
            def body(k, _):
                origin = lax.rem(me + count - k, count)
                copy(k, origin, origin).wait()
                return 0

            lax.fori_loop(1, count, body, 0)

        return start, finish

    pl.semaphore_wait(barrier, nf - 1 + nc - 1)
    gstart, gfinish = peers("curve", meta_ref, gath, gsend_sem, grecv_sem)
    gath[mc] = meta_ref[...]
    gstart()

    lane8 = lax.broadcasted_iota(jnp.int32, (BE, lanes), 1)
    lane64 = lax.broadcasted_iota(jnp.int32, (slab, lanes), 1)
    lane32 = lax.broadcasted_iota(jnp.int32, (slab // 2, lanes), 1)
    sub8 = lax.broadcasted_iota(jnp.int32, (BE, lanes), 0)

    rows, fishes, _ = mid_ref.shape
    width = tab.shape[1]
    for f in range(fishes):
        tab[0:rows, f * npts : (f + 1) * npts] = mid_ref[:, f, :]
    tab[rows:8, :] = jnp.zeros((8 - rows, width), F32)
    table = tab[...]
    for m in range(SEG):
        turned = table if m == 0 else pltpu.roll(table, width - m, axis=1)
        shifted[m * 8 : m * 8 + 8, :] = turned

    whole = inv_ref[...]
    hi = whole.astype(BF16)
    low = (whole - hi.astype(F32)).astype(BF16)
    for full, kept in ((hi, mh), (low, ml)):
        kept[0:slab, :] = full[0:slab, :]
        kept[slab : 2 * slab, :] = full[cells - slab :, :]
        kept[2 * slab :, :] = full[slab : cells - slab, :]

    def field_to_rows(read, out_ref):
        parts = []
        for g in range(group):
            bx, bz = g // bz_n, g % bz_n
            parts.append(read(bx, bz).reshape(slab, lanes))
        for j, rows in enumerate(swap_bits(parts, lane64)):
            out_ref[pl.ds(j, slab, stride=BE), :] = rows

    def rows_to_field(read_j, write):
        parts = swap_bits([read_j(j) for j in range(BE)], lane64)
        for bx in range(bx_n):
            for i in range(BE):
                plane = jnp.concatenate(
                    [parts[bx * bz_n + bz][i * BE : (i + 1) * BE, :] for bz in range(bz_n)], axis=0
                )
                write(bx * BE + i, plane)

    field_to_rows(
        lambda bx, bz: rs_ref[bx * BE : (bx + 1) * BE, bz * BE : (bz + 1) * BE, :], src
    )

    gfinish()

    col = lax.broadcasted_iota(jnp.int32, (lanes, lanes), 1)
    row = lax.broadcasted_iota(jnp.int32, (lanes, lanes), 0)
    earlier = jnp.where(row < col, 1.0, 0.0).astype(BF16)
    mine = gath[:, 2, :] == mc.astype(F32)
    rank = nn_dot(jnp.where(mine, 1.0, 0.0).astype(BF16), earlier)
    origin = lax.broadcasted_iota(jnp.int32, (nc, lanes), 0).astype(F32)
    slot = jnp.where(mine, origin * cap + rank, -1.0)
    rowf = row.astype(F32)
    picked = jnp.zeros((8, lanes), F32)
    for c in range(nc):
        hot = jnp.where(rowf == slot[c : c + 1, :], 1.0, 0.0).astype(BF16)
        picked = picked + nt_dot(gath[c].astype(BF16), hot)
    index = picked[0:1, :] * npts + picked[1:2, :]
    place = picked[3:4, :] - 1.0
    block_hot = jnp.where(rowf == place, 1.0, 0.0).astype(BF16)
    point_hot = jnp.where(
        lax.broadcasted_iota(jnp.int32, (width, lanes), 0).astype(F32) == index, 1.0, 0.0
    ).astype(BF16)
    hi, mid, low = split3(shifted[...])
    pt[...] = (nn_dot(hi, point_hot) + nn_dot(mid, point_hot)) + nn_dot(low, point_hot)

    cell = lax.broadcasted_iota(jnp.int32, (slab, lanes), 0)
    zc = (cell // BE).astype(F32) + 0.5
    yc = (cell % BE).astype(F32) + 0.5
    for m in range(SEG):
        dy = yc - pt[m * 8 + 1 : m * 8 + 2, :]
        dz = zc - pt[m * 8 + 2 : m * 8 + 3, :]
        dyz[m] = dy * dy + dz * dz

    half = slab // 2

    def build(i, _):
        xc = i.astype(F32) + 0.5
        for h in range(2):
            lo_row = h * half
            near = ws = vx = vy = vz = None
            for m in range(SEG):
                dx = xc - pt[m * 8 : m * 8 + 1, :]
                d = dyz[m, lo_row : lo_row + half, :] + dx * dx
                e = d + 0.25
                signed = e * lax.rsqrt(e) - pt[m * 8 + 6 : m * 8 + 7, :]
                a = 1.0 / (1.0 + d)
                ax = a * pt[m * 8 + 3 : m * 8 + 4, :]
                ay = a * pt[m * 8 + 4 : m * 8 + 5, :]
                az = a * pt[m * 8 + 5 : m * 8 + 6, :]
                if m == 0:
                    near, ws, vx, vy, vz = signed, a, ax, ay, az
                else:
                    near = jnp.minimum(near, signed)
                    ws, vx, vy, vz = ws + a, vx + ax, vy + ay, vz + az
            ind = 0.5 - 0.5 * jnp.tanh(near)
            scale = 1.0 / ws
            pay = jnp.concatenate(
                [ind, ind * (vx * scale), ind * (vy * scale), ind * (vz * scale)], axis=0
            ).astype(BF16)
            summed = nt_dot(pay, block_hot).astype(BF16).astype(F32)
            base = pl.multiple_of(i * slab + lo_row, half)
            for c in range(4):
                ob[c, pl.ds(base, half), :] = summed[c * half : (c + 1) * half, :]
        return 0

    lax.fori_loop(0, BE, build, 0)
    diag[...] = 6.0 + PENALTY * ob[0]
    src[...] = src[...] - ((ob[1] + ob[2]) + ob[3])

    def product(a, b):
        wide = nn_dot(mh[a:b, :], rhs[...])
        return (wide[:, :lanes] + wide[:, lanes:]) + nn_dot(ml[a:b, :], rhs[:, :lanes])

    bz8 = lane8 % bz_n
    bx8 = (lane8 // bz_n) % bx_n
    bx64 = (lane64 // bz_n) % bx_n
    bx32 = (lane32 // bz_n) % bx_n

    def turn(x, shift):
        shift = shift % lanes
        return x if shift == 0 else pltpu.roll(x, shift, axis=1)

    def halo(turn_no):
        def copy(buf, dst, k, device):
            return pltpu.make_async_remote_copy(
                src_ref=buf,
                dst_ref=dst.at[turn_no],
                send_sem=hsend_sem.at[turn_no, k],
                recv_sem=hrecv_sem.at[turn_no, k],
                device_id=device,
                device_id_type=MESH,
            )

        down_c = copy(xsend.at[turn_no, 0], xhigh, 0, (mf, lax.max(mc - 1, 0)))
        up_c = copy(xsend.at[turn_no, 1], xlow, 1, (mf, lax.min(mc + 1, nc - 1)))
        down_f = copy(zsend.at[turn_no, 0], zhigh, 2, (lax.max(mf - 1, 0), mc))
        up_f = copy(zsend.at[turn_no, 1], zlow, 3, (lax.min(mf + 1, nf - 1), mc))
        return down_c, up_c, down_f, up_f

    def apply(value, v_ref, out_ref, turn_no, between=None):
        down_c, up_c, down_f, up_f = halo(turn_no)
        has = (mc > 0, mc < nc - 1, mf > 0, mf < nf - 1)
        vh = value.astype(BF16)
        rhs[:, :lanes] = vh
        rhs[:, lanes:] = (value - vh.astype(F32)).astype(BF16)
        ends = product(0, 2 * slab)
        v0, v7 = ends[:slab], ends[slab:]
        v_ref[0:slab, :] = v0
        v_ref[cells - slab : cells, :] = v7
        xsend[turn_no, 0] = jnp.where(bx32 == 0, v0[:half], turn(v0[half:], bz_n))
        xsend[turn_no, 1] = jnp.where(bx32 == 0, turn(v7[:half], -bz_n), v7[half:])
        for cond, cp in zip(has[:2], (down_c, up_c)):
            pl.when(cond)(cp.start)
        v_ref[slab : cells - slab, :] = product(2 * slab, cells)
        for t in range(2):
            lowp = highp = None
            for a in range(bz_n):
                start = (t * bz_n + a) * slab
                lo = turn(v_ref[start : start + BE, :], a)
                hg = turn(v_ref[start + slab - BE : start + slab, :], a - (bz_n - 1))
                lowp = lo if a == 0 else jnp.where(bz8 == a, lo, lowp)
                highp = hg if a == 0 else jnp.where(bz8 == a, hg, highp)
            zsend[turn_no, 0, t * BE : (t + 1) * BE, :] = lowp
            zsend[turn_no, 1, t * BE : (t + 1) * BE, :] = highp
        for cond, cp in zip(has[2:], (down_f, up_f)):
            pl.when(cond)(cp.start)
        if between is not None:
            between()

        v0 = v_ref[0:slab, :]
        v7 = v_ref[cells - slab : cells, :]
        for i in range(BE):
            v = v_ref[i * slab : (i + 1) * slab, :]
            if i > 0:
                beside = v_ref[(i - 1) * slab : i * slab, :]
            else:
                beside = jnp.where(bx64 > 0, turn(v7, bz_n), 0.0)
            if i < BE - 1:
                beside = beside + v_ref[(i + 1) * slab : (i + 2) * slab, :]
            else:
                beside = beside + jnp.where(bx64 < bx_n - 1, turn(v0, -bz_n), 0.0)
            rows = []
            for k in range(BE):
                t = v[k * BE : (k + 1) * BE, :]
                if k > 0:
                    s = v[(k - 1) * BE : k * BE, :]
                else:
                    s = jnp.where(bz8 > 0, turn(v[slab - BE :, :], 1), 0.0)
                if k < BE - 1:
                    s = s + v[(k + 1) * BE : (k + 2) * BE, :]
                else:
                    s = s + jnp.where(bz8 < bz_n - 1, turn(v[:BE, :], -1), 0.0)
                down = pltpu.roll(t, 1, axis=0)
                edge = jnp.where(lane8 < group, 0.0, turn(down, group))
                s = s + jnp.where(sub8 == 0, edge, down)
                up = pltpu.roll(t, BE - 1, axis=0)
                edge = jnp.where(lane8 >= lanes - group, 0.0, turn(up, -group))
                s = s + jnp.where(sub8 == BE - 1, edge, up)
                rows.append(s)
            beside = beside + jnp.concatenate(rows, axis=0)
            out_ref[i * slab : (i + 1) * slab, :] = (
                diag[i * slab : (i + 1) * slab, :] * v - beside
            )

        for cond, cp in zip((has[1], has[0], has[3], has[2]), (down_c, up_c, down_f, up_f)):
            pl.when(cond)(cp.wait_recv)
        for cond, cp in zip(has, (down_c, up_c, down_f, up_f)):
            pl.when(cond)(cp.wait_send)

        got = xhigh[turn_no]
        for h, part in enumerate((turn(got, bz_n), got)):
            a = cells - slab + h * half
            out_ref[a : a + half, :] = out_ref[a : a + half, :] - jnp.where(
                bx32 == bx_n - 1, part, 0.0
            )
        got = xlow[turn_no]
        for h, part in enumerate((got, turn(got, -bz_n))):
            a = h * half
            out_ref[a : a + half, :] = out_ref[a : a + half, :] - jnp.where(bx32 == 0, part, 0.0)
        for t in range(2):
            gl = zlow[turn_no, t * BE : (t + 1) * BE, :]
            gh = zhigh[turn_no, t * BE : (t + 1) * BE, :]
            for a in range(bz_n):
                start = (t * bz_n + a) * slab
                out_ref[start : start + BE, :] = out_ref[start : start + BE, :] - jnp.where(
                    bz8 == 0, turn(gl, -a), 0.0
                )
                b = start + slab - BE
                out_ref[b : b + BE, :] = out_ref[b : b + BE, :] - jnp.where(
                    bz8 == bz_n - 1, turn(gh, bz_n - 1 - a), 0.0
                )

    def pack(pairs):
        rows = [jnp.sum(a * b, axis=0, keepdims=True) for a, b in pairs]
        rows += [jnp.zeros((1, lanes), F32)] * (8 - len(rows))
        return jnp.concatenate(rows, axis=0)

    def reduction(no):
        fstart, ffinish = peers(
            "fish", rsend.at[no, 0], rfish.at[no], fsend_sem.at[no], frecv_sem.at[no]
        )
        cstart, cfinish = peers(
            "curve", rsend.at[no, 1], rcurve.at[no], csend_sem.at[no], crecv_sem.at[no]
        )

        def first(tile):
            rsend[no, 0] = tile
            rfish[no, mf] = tile
            fstart()

        def second():
            ffinish()
            tile = jnp.sum(rfish[no], axis=0)
            rsend[no, 1] = tile
            rcurve[no, mc] = tile
            cstart()

        def last():
            cfinish()
            tile = jnp.sum(rcurve[no], axis=0)
            total = jnp.sum(tile, axis=1, keepdims=True)
            return [total[r : r + 1, :] for r in range(8)]

        return first, second, last

    apply(src[...], y1, v1, 0)
    apply(v1[...], m1, w1, 1)
    first, second, last = reduction(0)
    r, v, w = src[...], v1[...], w1[...]
    first(pack([(r, r), (r, v), (v, v), (v, w), (w, w), (r, w)]))
    apply(w1[...], n1, u1, 2, second)
    for c in range(4):
        def write(x, plane, c=c):
            obst_ref[c, x] = plane.astype(BF16)

        rows_to_field(lambda j, c=c: ob[c, pl.ds(j, slab, stride=BE), :], write)
    rr, rv, vv, vw, ww, rw, _, _ = last()
    alpha = rr / rv
    ts = (rv - alpha * vv) - alpha * (rw - alpha * vw)
    tt = (vv - alpha * vw) - alpha * (vw - alpha * ww)
    omega = ts / tt
    rho2 = (rr - alpha * rv) - omega * (rv - alpha * rw)
    beta = rho2 / rr * (alpha / omega)

    both, prod = alpha + omega, alpha * omega
    r = src[...]
    v, w = v1[...], w1[...]
    r2 = r - both * v + prod * w
    q = v - both * w + prod * u1[...]
    v2 = q + beta * (v - omega * w)
    mr2 = y1[...] - both * m1[...] + prod * n1[...]
    y2 = mr2 + beta * (y1[...] - omega * m1[...])
    n1[...] = alpha * y1[...] + omega * (y1[...] - alpha * m1[...])
    diag_keep = diag
    y1[...] = y2
    m1[...] = mr2
    w1[...] = r2
    u1[...] = q
    v1[...] = v2
    apply(v2, m2, w2, 3)
    r2, q, v2, w = w1[...], u1[...], v1[...], w2[...]
    first, second, last = reduction(1)
    first(
        pack([(src[...], v2), (q, r2), (q, v2), (w, r2), (w, v2), (q, q), (q, w), (w, w)])
    )
    second()
    sv, qr, qv, wr, wv, qq, qw, ww = last()
    alpha2 = rho2 / sv
    ts = (qr - alpha2 * qv) - alpha2 * (wr - alpha2 * wv)
    tt = (qq - alpha2 * qw) - alpha2 * (qw - alpha2 * ww)
    omega2 = ts / tt
    src[...] = n1[...] + alpha2 * y1[...] + omega2 * (m1[...] - alpha2 * m2[...])
    diag_keep[...] = (w1[...] - alpha2 * v1[...]) - omega2 * (u1[...] - alpha2 * w2[...])

    def write_press(x, plane):
        press_ref[x] = plane

    def write_resid(x, plane):
        resid_ref[x] = plane

    rows_to_field(lambda j: src[pl.ds(j, slab, stride=BE), :], write_press)
    rows_to_field(lambda j: diag_keep[pl.ds(j, slab, stride=BE), :], write_resid)


def local(right_side, block_inverse, midline, entry_fish, entry_seg, entry_dest, entry_block):
    nf, nc = lax.axis_size("fish"), lax.axis_size("curve")
    count = entry_fish.shape[0]
    cap = max(2, 2 * count // nc)
    cx, cz, ny = right_side.shape
    lanes = (cx // BE) * (cz // BE) * (ny // BE)
    cells = BE**3
    slab = BE * BE
    rows, fishes, npts = midline.shape
    width = fishes * npts
    vmem = pl.BlockSpec(memory_space=pltpu.VMEM)
    big = pltpu.VMEM((cells, lanes), F32)
    dma = pltpu.SemaphoreType.DMA
    return pl.pallas_call(
        functools.partial(kernel, nf, nc, cap, npts),
        out_shape=(
            jax.ShapeDtypeStruct((cx, cz, ny), F32),
            jax.ShapeDtypeStruct((cx, cz, ny), F32),
            jax.ShapeDtypeStruct((4, cx, cz, ny), BF16),
        ),
        in_specs=[vmem] * 7,
        out_specs=(vmem, vmem, vmem),
        scratch_shapes=[
            pltpu.VMEM((cells, cells), BF16),
            pltpu.VMEM((cells, cells), BF16),
            pltpu.VMEM((cells, 2 * lanes), BF16),
            pltpu.VMEM((8, lanes), F32),
            pltpu.VMEM((8, width), F32),
            pltpu.VMEM((nc, 8, lanes), F32),
            pltpu.VMEM((SEG * 8, width), F32),
            pltpu.VMEM((SEG * 8, lanes), F32),
            pltpu.VMEM((SEG, slab, lanes), F32),
            pltpu.VMEM((4, cells, lanes), F32),
        ]
        + [big] * 10
        + [
            pltpu.VMEM((4, 2, slab // 2, lanes), F32),
            pltpu.VMEM((4, 2, 2 * BE, lanes), F32),
            pltpu.VMEM((4, slab // 2, lanes), F32),
            pltpu.VMEM((4, slab // 2, lanes), F32),
            pltpu.VMEM((4, 2 * BE, lanes), F32),
            pltpu.VMEM((4, 2 * BE, lanes), F32),
            pltpu.VMEM((2, 2, 8, lanes), F32),
            pltpu.VMEM((2, nf, 8, lanes), F32),
            pltpu.VMEM((2, nc, 8, lanes), F32),
            dma((nc,)),
            dma((nc,)),
            dma((4, 4)),
            dma((4, 4)),
            dma((2, nf)),
            dma((2, nf)),
            dma((2, nc)),
            dma((2, nc)),
        ],
        compiler_params=pltpu.CompilerParams(collective_id=0, has_side_effects=True),
    )(
        right_side,
        block_inverse,
        midline,
        *(e.reshape(1, count) for e in (entry_fish, entry_seg, entry_dest, entry_block)),
    )


def solution(mesh):
    return jax.shard_map(
        local,
        mesh=mesh,
        in_specs=(
            P("curve", "fish", None),
            P(),
            P(None, "fish", None),
            P(("fish", "curve")),
            P(("fish", "curve")),
            P(("fish", "curve"), None),
            P(("fish", "curve")),
        ),
        out_specs=(
            P("curve", "fish", None),
            P("curve", "fish", None),
            P(None, "curve", "fish", None),
        ),
        check_vma=False,
    )
```

```python
import functools
import jax
import jax.numpy as jnp
from jax import lax
from jax.experimental import pallas as pl
from jax.experimental.pallas import tpu as pltpu
from jax.sharding import PartitionSpec as P

BE = 8
SEG = 16
PENALTY = 4.0
F32 = jnp.float32
BF16 = jnp.bfloat16
MESH = pl.DeviceIdType.MESH


def nt_dot(a, b):
    return lax.dot_general(a, b, (((1,), (1,)), ((), ())), preferred_element_type=F32)


def nn_dot(a, b):
    return lax.dot_general(a, b, (((1,), (0,)), ((), ())), preferred_element_type=F32)


def split3(x):
    hi = x.astype(BF16)
    rest = x - hi.astype(F32)
    mid = rest.astype(BF16)
    low = (rest - mid.astype(F32)).astype(BF16)
    return hi, mid, low


def swap_bits(arrays, lane):
    arrays = list(arrays)
    lanes = lane.shape[-1]
    for step in (4, 2, 1):
        clear = (lane & step) == 0
        for a in range(8):
            if a & step:
                continue
            low, high = arrays[a], arrays[a | step]
            arrays[a] = jnp.where(clear, low, pltpu.roll(high, step, axis=1))
            arrays[a | step] = jnp.where(clear, pltpu.roll(low, lanes - step, axis=1), high)
    return arrays


def rows_to_field(read_j, write, bx_n, bz_n, lane):
    parts = swap_bits([read_j(j) for j in range(BE)], lane)
    for bx in range(bx_n):
        for i in range(BE):
            plane = jnp.concatenate(
                [parts[bx * bz_n + bz][i * BE : (i + 1) * BE, :] for bz in range(bz_n)], axis=0
            )
            write(bx * BE + i, plane)


def finish(
    prow_ref, rrow_ref, oin_ref, press_ref, resid_ref, obst_ref, prow, rrow, pf, rf, of, sems
):
    slab = BE * BE
    bx_n, bz_n = pf.shape[0] // BE, pf.shape[1] // BE
    lane = lax.broadcasted_iota(jnp.int32, (slab, prow.shape[1]), 1)
    take = [
        pltpu.make_async_copy(a, b, sems.at[n])
        for n, (a, b) in enumerate(((prow_ref, prow), (rrow_ref, rrow), (oin_ref, of)))
    ]
    give = [
        pltpu.make_async_copy(a, b, sems.at[3 + n])
        for n, (a, b) in enumerate(((pf, press_ref), (rf, resid_ref), (of, obst_ref)))
    ]
    for copy in take:
        copy.start()
    for n, (rows, field) in enumerate(((prow, pf), (rrow, rf))):
        take[n].wait()

        def write(x, plane, field=field):
            field[x] = plane

        rows_to_field(
            lambda j, rows=rows: rows[pl.ds(j, slab, stride=BE), :], write, bx_n, bz_n, lane
        )
        give[n].start()
        if n == 0:
            take[2].wait()
            give[2].start()
    for copy in give:
        copy.wait()


def kernel(
    nf, nc, cap, npts,
    rs_ref, inv_ref, mid_ref, fish_ref, seg_ref, dest_ref, block_ref,
    press_ref, resid_ref, obst_ref,
    obf, obf_sem, mh, ml, rhs, meta_ref, tab, gath, shifted, pt, dyz, ob, src, diag,
    y1, v1, m1, w1, n1, u1, m2, w2,
    xsend, zsend, xlow, xhigh, zlow, zhigh, rsend, rfish, rcurve,
    gsend_sem, grecv_sem, hsend_sem, hrecv_sem, fsend_sem, frecv_sem, csend_sem, crecv_sem,
):
    mf = lax.axis_index("fish")
    mc = lax.axis_index("curve")
    cells, lanes = src.shape
    slab = BE * BE
    bx_n = rs_ref.shape[0] // BE
    bz_n = rs_ref.shape[1] // BE
    group = bx_n * bz_n

    barrier = pltpu.get_barrier_semaphore()

    def greet_fish(k, _):
        pl.semaphore_signal(
            barrier, inc=1, device_id=(lax.rem(mf + k, nf), mc), device_id_type=MESH
        )
        return 0

    def greet_curve(k, _):
        pl.semaphore_signal(
            barrier, inc=1, device_id=(mf, lax.rem(mc + k, nc)), device_id_type=MESH
        )
        return 0

    nyb = rs_ref.shape[2] // BE
    count = fish_ref.shape[1]
    meta_ref[...] = jnp.full_like(meta_ref, -1.0)
    block = block_ref[...]
    place_in = block % nyb * group + block // nyb + 1
    for r, column in enumerate((fish_ref[...], seg_ref[...], dest_ref[...], place_in)):
        meta_ref[r : r + 1, 0:count] = column.astype(F32)
    xlow[...] = jnp.zeros_like(xlow)
    xhigh[...] = jnp.zeros_like(xhigh)
    zlow[...] = jnp.zeros_like(zlow)
    zhigh[...] = jnp.zeros_like(zhigh)
    lax.fori_loop(1, nf, greet_fish, 0)
    lax.fori_loop(1, nc, greet_curve, 0)

    def peers(axis, src_at, dst, send_sem, recv_sem):
        count = nf if axis == "fish" else nc
        me = mf if axis == "fish" else mc

        def copy(k, slot, target):
            device = (target, mc) if axis == "fish" else (mf, target)
            return pltpu.make_async_remote_copy(
                src_ref=src_at,
                dst_ref=dst.at[slot],
                send_sem=send_sem.at[k],
                recv_sem=recv_sem.at[k],
                device_id=device,
                device_id_type=MESH,
            )

        def start():
            def body(k, _):
                copy(k, me, lax.rem(me + k, count)).start()
                return 0

            lax.fori_loop(1, count, body, 0)

        def finish():
            def body(k, _):
                origin = lax.rem(me + count - k, count)
                copy(k, origin, origin).wait()
                return 0

            lax.fori_loop(1, count, body, 0)

        return start, finish

    pl.semaphore_wait(barrier, nf - 1 + nc - 1)
    gstart, gfinish = peers("curve", meta_ref, gath, gsend_sem, grecv_sem)
    gath[mc] = meta_ref[...]
    gstart()

    lane8 = lax.broadcasted_iota(jnp.int32, (BE, lanes), 1)
    lane64 = lax.broadcasted_iota(jnp.int32, (slab, lanes), 1)
    lane32 = lax.broadcasted_iota(jnp.int32, (slab // 2, lanes), 1)
    sub8 = lax.broadcasted_iota(jnp.int32, (BE, lanes), 0)

    rows, fishes, _ = mid_ref.shape
    width = tab.shape[1]
    for f in range(fishes):
        tab[0:rows, f * npts : (f + 1) * npts] = mid_ref[:, f, :]
    tab[rows:8, :] = jnp.zeros((8 - rows, width), F32)
    table = tab[...]
    for m in range(SEG):
        turned = table if m == 0 else pltpu.roll(table, width - m, axis=1)
        shifted[m * 8 : m * 8 + 8, :] = turned

    whole = inv_ref[...]
    hi = whole.astype(BF16)
    low = (whole - hi.astype(F32)).astype(BF16)
    for full, kept in ((hi, mh), (low, ml)):
        kept[0:slab, :] = full[0:slab, :]
        kept[slab : 2 * slab, :] = full[cells - slab :, :]
        kept[2 * slab :, :] = full[slab : cells - slab, :]

    def field_to_rows(read, out_ref):
        parts = []
        for g in range(group):
            bx, bz = g // bz_n, g % bz_n
            parts.append(read(bx, bz).reshape(slab, lanes))
        for j, rows in enumerate(swap_bits(parts, lane64)):
            out_ref[pl.ds(j, slab, stride=BE), :] = rows

    field_to_rows(
        lambda bx, bz: rs_ref[bx * BE : (bx + 1) * BE, bz * BE : (bz + 1) * BE, :], src
    )

    gfinish()

    col = lax.broadcasted_iota(jnp.int32, (lanes, lanes), 1)
    row = lax.broadcasted_iota(jnp.int32, (lanes, lanes), 0)
    earlier = jnp.where(row < col, 1.0, 0.0).astype(BF16)
    mine = gath[:, 2, :] == mc.astype(F32)
    rank = nn_dot(jnp.where(mine, 1.0, 0.0).astype(BF16), earlier)
    origin = lax.broadcasted_iota(jnp.int32, (nc, lanes), 0).astype(F32)
    slot = jnp.where(mine, origin * cap + rank, -1.0)
    rowf = row.astype(F32)
    picked = jnp.zeros((8, lanes), F32)
    for c in range(nc):
        hot = jnp.where(rowf == slot[c : c + 1, :], 1.0, 0.0).astype(BF16)
        picked = picked + nt_dot(gath[c].astype(BF16), hot)
    index = picked[0:1, :] * npts + picked[1:2, :]
    place = picked[3:4, :] - 1.0
    block_hot = jnp.where(rowf == place, 1.0, 0.0).astype(BF16)
    point_hot = jnp.where(
        lax.broadcasted_iota(jnp.int32, (width, lanes), 0).astype(F32) == index, 1.0, 0.0
    ).astype(BF16)
    hi, mid, low = split3(shifted[...])
    pt[...] = (nn_dot(hi, point_hot) + nn_dot(mid, point_hot)) + nn_dot(low, point_hot)

    cell = lax.broadcasted_iota(jnp.int32, (slab, lanes), 0)
    zc = (cell // BE).astype(F32) + 0.5
    yc = (cell % BE).astype(F32) + 0.5
    for m in range(SEG):
        dy = yc - pt[m * 8 + 1 : m * 8 + 2, :]
        dz = zc - pt[m * 8 + 2 : m * 8 + 3, :]
        dyz[m] = dy * dy + dz * dz

    half = slab // 2

    def build(i, _):
        xc = i.astype(F32) + 0.5
        for h in range(2):
            lo_row = h * half
            near = ws = vx = vy = vz = None
            for m in range(SEG):
                dx = xc - pt[m * 8 : m * 8 + 1, :]
                d = dyz[m, lo_row : lo_row + half, :] + dx * dx
                e = d + 0.25
                signed = e * lax.rsqrt(e) - pt[m * 8 + 6 : m * 8 + 7, :]
                a = 1.0 / (1.0 + d)
                ax = a * pt[m * 8 + 3 : m * 8 + 4, :]
                ay = a * pt[m * 8 + 4 : m * 8 + 5, :]
                az = a * pt[m * 8 + 5 : m * 8 + 6, :]
                if m == 0:
                    near, ws, vx, vy, vz = signed, a, ax, ay, az
                else:
                    near = jnp.minimum(near, signed)
                    ws, vx, vy, vz = ws + a, vx + ax, vy + ay, vz + az
            ind = 0.5 - 0.5 * jnp.tanh(near)
            scale = 1.0 / ws
            pay = jnp.concatenate(
                [ind, ind * (vx * scale), ind * (vy * scale), ind * (vz * scale)], axis=0
            ).astype(BF16)
            summed = nt_dot(pay, block_hot).astype(BF16).astype(F32)
            base = pl.multiple_of(i * slab + lo_row, half)
            for c in range(4):
                ob[c, pl.ds(base, half), :] = summed[c * half : (c + 1) * half, :]
        return 0

    lax.fori_loop(0, BE, build, 0)
    diag[...] = 6.0 + PENALTY * ob[0]
    src[...] = src[...] - ((ob[1] + ob[2]) + ob[3])

    def product(a, b):
        wide = nn_dot(mh[a:b, :], rhs[...])
        return (wide[:, :lanes] + wide[:, lanes:]) + nn_dot(ml[a:b, :], rhs[:, :lanes])

    bz8 = lane8 % bz_n
    bx8 = (lane8 // bz_n) % bx_n
    bx64 = (lane64 // bz_n) % bx_n
    bx32 = (lane32 // bz_n) % bx_n

    def turn(x, shift):
        shift = shift % lanes
        return x if shift == 0 else pltpu.roll(x, shift, axis=1)

    def halo(turn_no):
        def copy(buf, dst, k, device):
            return pltpu.make_async_remote_copy(
                src_ref=buf,
                dst_ref=dst.at[turn_no],
                send_sem=hsend_sem.at[turn_no, k],
                recv_sem=hrecv_sem.at[turn_no, k],
                device_id=device,
                device_id_type=MESH,
            )

        down_c = copy(xsend.at[turn_no, 0], xhigh, 0, (mf, lax.max(mc - 1, 0)))
        up_c = copy(xsend.at[turn_no, 1], xlow, 1, (mf, lax.min(mc + 1, nc - 1)))
        down_f = copy(zsend.at[turn_no, 0], zhigh, 2, (lax.max(mf - 1, 0), mc))
        up_f = copy(zsend.at[turn_no, 1], zlow, 3, (lax.min(mf + 1, nf - 1), mc))
        return down_c, up_c, down_f, up_f

    def apply(value, v_ref, out_ref, turn_no, between=None):
        down_c, up_c, down_f, up_f = halo(turn_no)
        has = (mc > 0, mc < nc - 1, mf > 0, mf < nf - 1)
        vh = value.astype(BF16)
        rhs[:, :lanes] = vh
        rhs[:, lanes:] = (value - vh.astype(F32)).astype(BF16)
        ends = product(0, 2 * slab)
        v0, v7 = ends[:slab], ends[slab:]
        v_ref[0:slab, :] = v0
        v_ref[cells - slab : cells, :] = v7
        xsend[turn_no, 0] = jnp.where(bx32 == 0, v0[:half], turn(v0[half:], bz_n))
        xsend[turn_no, 1] = jnp.where(bx32 == 0, turn(v7[:half], -bz_n), v7[half:])
        for cond, cp in zip(has[:2], (down_c, up_c)):
            pl.when(cond)(cp.start)
        v_ref[slab : cells - slab, :] = product(2 * slab, cells)
        for t in range(2):
            lowp = highp = None
            for a in range(bz_n):
                start = (t * bz_n + a) * slab
                lo = turn(v_ref[start : start + BE, :], a)
                hg = turn(v_ref[start + slab - BE : start + slab, :], a - (bz_n - 1))
                lowp = lo if a == 0 else jnp.where(bz8 == a, lo, lowp)
                highp = hg if a == 0 else jnp.where(bz8 == a, hg, highp)
            zsend[turn_no, 0, t * BE : (t + 1) * BE, :] = lowp
            zsend[turn_no, 1, t * BE : (t + 1) * BE, :] = highp
        for cond, cp in zip(has[2:], (down_f, up_f)):
            pl.when(cond)(cp.start)
        if between is not None:
            between()

        v0 = v_ref[0:slab, :]
        v7 = v_ref[cells - slab : cells, :]
        for i in range(BE):
            v = v_ref[i * slab : (i + 1) * slab, :]
            if i > 0:
                beside = v_ref[(i - 1) * slab : i * slab, :]
            else:
                beside = jnp.where(bx64 > 0, turn(v7, bz_n), 0.0)
            if i < BE - 1:
                beside = beside + v_ref[(i + 1) * slab : (i + 2) * slab, :]
            else:
                beside = beside + jnp.where(bx64 < bx_n - 1, turn(v0, -bz_n), 0.0)
            rows = []
            for k in range(BE):
                t = v[k * BE : (k + 1) * BE, :]
                if k > 0:
                    s = v[(k - 1) * BE : k * BE, :]
                else:
                    s = jnp.where(bz8 > 0, turn(v[slab - BE :, :], 1), 0.0)
                if k < BE - 1:
                    s = s + v[(k + 1) * BE : (k + 2) * BE, :]
                else:
                    s = s + jnp.where(bz8 < bz_n - 1, turn(v[:BE, :], -1), 0.0)
                down = pltpu.roll(t, 1, axis=0)
                edge = jnp.where(lane8 < group, 0.0, turn(down, group))
                s = s + jnp.where(sub8 == 0, edge, down)
                up = pltpu.roll(t, BE - 1, axis=0)
                edge = jnp.where(lane8 >= lanes - group, 0.0, turn(up, -group))
                s = s + jnp.where(sub8 == BE - 1, edge, up)
                rows.append(s)
            beside = beside + jnp.concatenate(rows, axis=0)
            out_ref[i * slab : (i + 1) * slab, :] = (
                diag[i * slab : (i + 1) * slab, :] * v - beside
            )

        for cond, cp in zip((has[1], has[0], has[3], has[2]), (down_c, up_c, down_f, up_f)):
            pl.when(cond)(cp.wait_recv)
        for cond, cp in zip(has, (down_c, up_c, down_f, up_f)):
            pl.when(cond)(cp.wait_send)

        got = xhigh[turn_no]
        for h, part in enumerate((turn(got, bz_n), got)):
            a = cells - slab + h * half
            out_ref[a : a + half, :] = out_ref[a : a + half, :] - jnp.where(
                bx32 == bx_n - 1, part, 0.0
            )
        got = xlow[turn_no]
        for h, part in enumerate((got, turn(got, -bz_n))):
            a = h * half
            out_ref[a : a + half, :] = out_ref[a : a + half, :] - jnp.where(bx32 == 0, part, 0.0)
        for t in range(2):
            gl = zlow[turn_no, t * BE : (t + 1) * BE, :]
            gh = zhigh[turn_no, t * BE : (t + 1) * BE, :]
            for a in range(bz_n):
                start = (t * bz_n + a) * slab
                out_ref[start : start + BE, :] = out_ref[start : start + BE, :] - jnp.where(
                    bz8 == 0, turn(gl, -a), 0.0
                )
                b = start + slab - BE
                out_ref[b : b + BE, :] = out_ref[b : b + BE, :] - jnp.where(
                    bz8 == bz_n - 1, turn(gh, bz_n - 1 - a), 0.0
                )

    def pack(pairs):
        rows = [jnp.sum(a * b, axis=0, keepdims=True) for a, b in pairs]
        rows += [jnp.zeros((1, lanes), F32)] * (8 - len(rows))
        return jnp.concatenate(rows, axis=0)

    def reduction(no):
        fstart, ffinish = peers(
            "fish", rsend.at[no, 0], rfish.at[no], fsend_sem.at[no], frecv_sem.at[no]
        )
        cstart, cfinish = peers(
            "curve", rsend.at[no, 1], rcurve.at[no], csend_sem.at[no], crecv_sem.at[no]
        )

        def first(tile):
            rsend[no, 0] = tile
            rfish[no, mf] = tile
            fstart()

        def second():
            ffinish()
            tile = jnp.sum(rfish[no], axis=0)
            rsend[no, 1] = tile
            rcurve[no, mc] = tile
            cstart()

        def last():
            cfinish()
            tile = jnp.sum(rcurve[no], axis=0)
            total = jnp.sum(tile, axis=1, keepdims=True)
            return [total[r : r + 1, :] for r in range(8)]

        return first, second, last

    apply(src[...], y1, v1, 0)
    apply(v1[...], m1, w1, 1)
    first, second, last = reduction(0)
    r, v, w = src[...], v1[...], w1[...]
    first(pack([(r, r), (r, v), (v, v), (v, w), (w, w), (r, w)]))
    apply(w1[...], n1, u1, 2, second)
    for c in range(4):
        def write(x, plane, c=c):
            obf[c, x] = plane.astype(BF16)

        rows_to_field(
            lambda j, c=c: ob[c, pl.ds(j, slab, stride=BE), :], write, bx_n, bz_n, lane64
        )
    out_copy = pltpu.make_async_copy(obf, obst_ref, obf_sem)
    out_copy.start()
    rr, rv, vv, vw, ww, rw, _, _ = last()
    alpha = rr / rv
    ts = (rv - alpha * vv) - alpha * (rw - alpha * vw)
    tt = (vv - alpha * vw) - alpha * (vw - alpha * ww)
    omega = ts / tt
    rho2 = (rr - alpha * rv) - omega * (rv - alpha * rw)
    beta = rho2 / rr * (alpha / omega)

    both, prod = alpha + omega, alpha * omega
    r = src[...]
    v, w = v1[...], w1[...]
    r2 = r - both * v + prod * w
    q = v - both * w + prod * u1[...]
    v2 = q + beta * (v - omega * w)
    mr2 = y1[...] - both * m1[...] + prod * n1[...]
    y2 = mr2 + beta * (y1[...] - omega * m1[...])
    n1[...] = alpha * y1[...] + omega * (y1[...] - alpha * m1[...])
    y1[...] = y2
    m1[...] = mr2
    w1[...] = r2
    u1[...] = q
    v1[...] = v2
    apply(v2, m2, w2, 3)
    r2, q, v2, w = w1[...], u1[...], v1[...], w2[...]
    first, second, last = reduction(1)
    first(
        pack([(src[...], v2), (q, r2), (q, v2), (w, r2), (w, v2), (q, q), (q, w), (w, w)])
    )
    second()
    sv, qr, qv, wr, wv, qq, qw, ww = last()
    alpha2 = rho2 / sv
    ts = (qr - alpha2 * qv) - alpha2 * (wr - alpha2 * wv)
    tt = (qq - alpha2 * qw) - alpha2 * (qw - alpha2 * ww)
    omega2 = ts / tt
    press_ref[...] = n1[...] + alpha2 * y1[...] + omega2 * (m1[...] - alpha2 * m2[...])
    resid_ref[...] = (w1[...] - alpha2 * v1[...]) - omega2 * (u1[...] - alpha2 * w2[...])
    out_copy.wait()


def local(right_side, block_inverse, midline, entry_fish, entry_seg, entry_dest, entry_block):
    nf, nc = lax.axis_size("fish"), lax.axis_size("curve")
    count = entry_fish.shape[0]
    cap = max(2, 2 * count // nc)
    cx, cz, ny = right_side.shape
    lanes = (cx // BE) * (cz // BE) * (ny // BE)
    cells = BE**3
    slab = BE * BE
    rows, fishes, npts = midline.shape
    width = fishes * npts
    vmem = pl.BlockSpec(memory_space=pltpu.VMEM)
    big = pltpu.VMEM((cells, lanes), F32)
    dma = pltpu.SemaphoreType.DMA
    anywhere = pl.BlockSpec(memory_space=pl.ANY)
    field = jax.ShapeDtypeStruct((cx, cz, ny), F32)
    fields = jax.ShapeDtypeStruct((4, cx, cz, ny), BF16)
    row_form = jax.ShapeDtypeStruct((cells, lanes), F32)
    solved = pl.pallas_call(
        functools.partial(kernel, nf, nc, cap, npts),
        out_shape=(row_form, row_form, fields),
        in_specs=[vmem] * 7,
        out_specs=(vmem, vmem, anywhere),
        scratch_shapes=[
            pltpu.VMEM((4, cx, cz, ny), BF16),
            dma,
            pltpu.VMEM((cells, cells), BF16),
            pltpu.VMEM((cells, cells), BF16),
            pltpu.VMEM((cells, 2 * lanes), BF16),
            pltpu.VMEM((8, lanes), F32),
            pltpu.VMEM((8, width), F32),
            pltpu.VMEM((nc, 8, lanes), F32),
            pltpu.VMEM((SEG * 8, width), F32),
            pltpu.VMEM((SEG * 8, lanes), F32),
            pltpu.VMEM((SEG, slab, lanes), F32),
            pltpu.VMEM((4, cells, lanes), F32),
        ]
        + [big] * 10
        + [
            pltpu.VMEM((4, 2, slab // 2, lanes), F32),
            pltpu.VMEM((4, 2, 2 * BE, lanes), F32),
            pltpu.VMEM((4, slab // 2, lanes), F32),
            pltpu.VMEM((4, slab // 2, lanes), F32),
            pltpu.VMEM((4, 2 * BE, lanes), F32),
            pltpu.VMEM((4, 2 * BE, lanes), F32),
            pltpu.VMEM((2, 2, 8, lanes), F32),
            pltpu.VMEM((2, nf, 8, lanes), F32),
            pltpu.VMEM((2, nc, 8, lanes), F32),
            dma((nc,)),
            dma((nc,)),
            dma((4, 4)),
            dma((4, 4)),
            dma((2, nf)),
            dma((2, nf)),
            dma((2, nc)),
            dma((2, nc)),
        ],
        compiler_params=pltpu.CompilerParams(collective_id=0, has_side_effects=True),
    )(
        right_side,
        block_inverse,
        midline,
        *(e.reshape(1, count) for e in (entry_fish, entry_seg, entry_dest, entry_block)),
    )
    return pl.pallas_call(
        finish,
        out_shape=(field, field, fields),
        in_specs=[anywhere] * 3,
        out_specs=(anywhere,) * 3,
        scratch_shapes=[
            big,
            big,
            pltpu.VMEM((cx, cz, ny), F32),
            pltpu.VMEM((cx, cz, ny), F32),
            pltpu.VMEM((4, cx, cz, ny), BF16),
            dma((6,)),
        ],
    )(*solved)


def solution(mesh):
    return jax.shard_map(
        local,
        mesh=mesh,
        in_specs=(
            P("curve", "fish", None),
            P(),
            P(None, "fish", None),
            P(("fish", "curve")),
            P(("fish", "curve")),
            P(("fish", "curve"), None),
            P(("fish", "curve")),
        ),
        out_specs=(
            P("curve", "fish", None),
            P("curve", "fish", None),
            P(None, "curve", "fish", None),
        ),
        check_vma=False,
    )
```

```python
import functools
import jax
import jax.numpy as jnp
from jax import lax
from jax.experimental import pallas as pl
from jax.experimental.pallas import tpu as pltpu
from jax.sharding import PartitionSpec as P

BE = 8
SEG = 16
PENALTY = 4.0
F32 = jnp.float32
BF16 = jnp.bfloat16
MESH = pl.DeviceIdType.MESH


def nt_dot(a, b):
    return lax.dot_general(a, b, (((1,), (1,)), ((), ())), preferred_element_type=F32)


def nn_dot(a, b):
    return lax.dot_general(a, b, (((1,), (0,)), ((), ())), preferred_element_type=F32)


def split3(x):
    hi = x.astype(BF16)
    rest = x - hi.astype(F32)
    mid = rest.astype(BF16)
    low = (rest - mid.astype(F32)).astype(BF16)
    return hi, mid, low


def swap_bits(arrays, lane):
    arrays = list(arrays)
    lanes = lane.shape[-1]
    for step in (4, 2, 1):
        clear = (lane & step) == 0
        for a in range(8):
            if a & step:
                continue
            low, high = arrays[a], arrays[a | step]
            arrays[a] = jnp.where(clear, low, pltpu.roll(high, step, axis=1))
            arrays[a | step] = jnp.where(clear, pltpu.roll(low, lanes - step, axis=1), high)
    return arrays


def rows_to_field(read_j, write, bx_n, bz_n, lane):
    parts = swap_bits([read_j(j) for j in range(BE)], lane)
    for bx in range(bx_n):
        for i in range(BE):
            plane = jnp.concatenate(
                [parts[bx * bz_n + bz][i * BE : (i + 1) * BE, :] for bz in range(bz_n)], axis=0
            )
            write(bx * BE + i, plane)


def finish(
    prow_ref, rrow_ref, oin_ref, press_ref, resid_ref, obst_ref, prow, rrow, pf, rf, of, sems
):
    slab = BE * BE
    bx_n, bz_n = pf.shape[0] // BE, pf.shape[1] // BE
    lane = lax.broadcasted_iota(jnp.int32, (slab, prow.shape[1]), 1)
    take = [
        pltpu.make_async_copy(a, b, sems.at[n])
        for n, (a, b) in enumerate(((prow_ref, prow), (rrow_ref, rrow), (oin_ref, of)))
    ]
    give = [
        pltpu.make_async_copy(a, b, sems.at[3 + n])
        for n, (a, b) in enumerate(((pf, press_ref), (rf, resid_ref), (of, obst_ref)))
    ]
    for copy in take:
        copy.start()
    for n, (rows, field) in enumerate(((prow, pf), (rrow, rf))):
        take[n].wait()

        def write(x, plane, field=field):
            field[x] = plane

        rows_to_field(
            lambda j, rows=rows: rows[pl.ds(j, slab, stride=BE), :], write, bx_n, bz_n, lane
        )
        give[n].start()
        if n == 0:
            take[2].wait()
            give[2].start()
    for copy in give:
        copy.wait()


def kernel(
    nf, nc, cap, npts,
    rs_hbm, inv_hbm, mid_ref, fish_ref, seg_ref, dest_ref, block_ref,
    press_hbm, resid_hbm, obst_ref,
    rs_ref, inv_ref, in_sem, obf, obf_sem, mh, ml, rhs, meta_ref, tab, gath, shifted, pt, dyz, ob, src, diag,
    y1, v1, m1, w1, n1, u1, m2, w2,
    xsend, zsend, xlow, xhigh, zlow, zhigh, rsend, rfish, rcurve,
    gsend_sem, grecv_sem, hsend_sem, hrecv_sem, fsend_sem, frecv_sem, csend_sem, crecv_sem,
):
    mf = lax.axis_index("fish")
    mc = lax.axis_index("curve")
    cells, lanes = src.shape
    slab = BE * BE
    bx_n = rs_ref.shape[0] // BE
    bz_n = rs_ref.shape[1] // BE
    group = bx_n * bz_n

    inv_copy = pltpu.make_async_copy(inv_hbm, inv_ref, in_sem.at[0])
    rs_copy = pltpu.make_async_copy(rs_hbm, rs_ref, in_sem.at[1])
    inv_copy.start()
    rs_copy.start()

    barrier = pltpu.get_barrier_semaphore()

    def greet_fish(k, _):
        pl.semaphore_signal(
            barrier, inc=1, device_id=(lax.rem(mf + k, nf), mc), device_id_type=MESH
        )
        return 0

    def greet_curve(k, _):
        pl.semaphore_signal(
            barrier, inc=1, device_id=(mf, lax.rem(mc + k, nc)), device_id_type=MESH
        )
        return 0

    nyb = rs_ref.shape[2] // BE
    count = fish_ref.shape[1]
    meta_ref[...] = jnp.full_like(meta_ref, -1.0)
    block = block_ref[...]
    place_in = block % nyb * group + block // nyb + 1
    for r, column in enumerate((fish_ref[...], seg_ref[...], dest_ref[...], place_in)):
        meta_ref[r : r + 1, 0:count] = column.astype(F32)
    xlow[...] = jnp.zeros_like(xlow)
    xhigh[...] = jnp.zeros_like(xhigh)
    zlow[...] = jnp.zeros_like(zlow)
    zhigh[...] = jnp.zeros_like(zhigh)
    lax.fori_loop(1, nf, greet_fish, 0)
    lax.fori_loop(1, nc, greet_curve, 0)

    def peers(axis, src_at, dst, send_sem, recv_sem):
        count = nf if axis == "fish" else nc
        me = mf if axis == "fish" else mc

        def copy(k, slot, target):
            device = (target, mc) if axis == "fish" else (mf, target)
            return pltpu.make_async_remote_copy(
                src_ref=src_at,
                dst_ref=dst.at[slot],
                send_sem=send_sem.at[k],
                recv_sem=recv_sem.at[k],
                device_id=device,
                device_id_type=MESH,
            )

        def start():
            def body(k, _):
                copy(k, me, lax.rem(me + k, count)).start()
                return 0

            lax.fori_loop(1, count, body, 0)

        def finish():
            def body(k, _):
                origin = lax.rem(me + count - k, count)
                copy(k, origin, origin).wait()
                return 0

            lax.fori_loop(1, count, body, 0)

        return start, finish

    pl.semaphore_wait(barrier, nf - 1 + nc - 1)
    gstart, gfinish = peers("curve", meta_ref, gath, gsend_sem, grecv_sem)
    gath[mc] = meta_ref[...]
    gstart()

    lane8 = lax.broadcasted_iota(jnp.int32, (BE, lanes), 1)
    lane64 = lax.broadcasted_iota(jnp.int32, (slab, lanes), 1)
    lane32 = lax.broadcasted_iota(jnp.int32, (slab // 2, lanes), 1)
    sub8 = lax.broadcasted_iota(jnp.int32, (BE, lanes), 0)

    rows, fishes, _ = mid_ref.shape
    width = tab.shape[1]
    for f in range(fishes):
        tab[0:rows, f * npts : (f + 1) * npts] = mid_ref[:, f, :]
    tab[rows:8, :] = jnp.zeros((8 - rows, width), F32)
    table = tab[...]
    for m in range(SEG):
        turned = table if m == 0 else pltpu.roll(table, width - m, axis=1)
        shifted[m * 8 : m * 8 + 8, :] = turned

    inv_copy.wait()
    whole = inv_ref[...]
    hi = whole.astype(BF16)
    low = (whole - hi.astype(F32)).astype(BF16)
    for full, kept in ((hi, mh), (low, ml)):
        kept[0:slab, :] = full[0:slab, :]
        kept[slab : 2 * slab, :] = full[cells - slab :, :]
        kept[2 * slab :, :] = full[slab : cells - slab, :]

    def field_to_rows(read, out_ref):
        parts = []
        for g in range(group):
            bx, bz = g // bz_n, g % bz_n
            parts.append(read(bx, bz).reshape(slab, lanes))
        for j, rows in enumerate(swap_bits(parts, lane64)):
            out_ref[pl.ds(j, slab, stride=BE), :] = rows

    rs_copy.wait()
    field_to_rows(
        lambda bx, bz: rs_ref[bx * BE : (bx + 1) * BE, bz * BE : (bz + 1) * BE, :], src
    )

    gfinish()

    col = lax.broadcasted_iota(jnp.int32, (lanes, lanes), 1)
    row = lax.broadcasted_iota(jnp.int32, (lanes, lanes), 0)
    earlier = jnp.where(row < col, 1.0, 0.0).astype(BF16)
    mine = gath[:, 2, :] == mc.astype(F32)
    rank = nn_dot(jnp.where(mine, 1.0, 0.0).astype(BF16), earlier)
    origin = lax.broadcasted_iota(jnp.int32, (nc, lanes), 0).astype(F32)
    slot = jnp.where(mine, origin * cap + rank, -1.0)
    rowf = row.astype(F32)
    picked = jnp.zeros((8, lanes), F32)
    for c in range(nc):
        hot = jnp.where(rowf == slot[c : c + 1, :], 1.0, 0.0).astype(BF16)
        picked = picked + nt_dot(gath[c].astype(BF16), hot)
    index = picked[0:1, :] * npts + picked[1:2, :]
    place = picked[3:4, :] - 1.0
    block_hot = jnp.where(rowf == place, 1.0, 0.0).astype(BF16)
    point_hot = jnp.where(
        lax.broadcasted_iota(jnp.int32, (width, lanes), 0).astype(F32) == index, 1.0, 0.0
    ).astype(BF16)
    hi, mid, low = split3(shifted[...])
    pt[...] = (nn_dot(hi, point_hot) + nn_dot(mid, point_hot)) + nn_dot(low, point_hot)

    cell = lax.broadcasted_iota(jnp.int32, (slab, lanes), 0)
    zc = (cell // BE).astype(F32) + 0.5
    yc = (cell % BE).astype(F32) + 0.5
    for m in range(SEG):
        dy = yc - pt[m * 8 + 1 : m * 8 + 2, :]
        dz = zc - pt[m * 8 + 2 : m * 8 + 3, :]
        dyz[m] = dy * dy + dz * dz

    half = slab // 2

    def build(i, _):
        xc = i.astype(F32) + 0.5
        for h in range(2):
            lo_row = h * half
            near = ws = vx = vy = vz = None
            for m in range(SEG):
                dx = xc - pt[m * 8 : m * 8 + 1, :]
                d = dyz[m, lo_row : lo_row + half, :] + dx * dx
                e = d + 0.25
                signed = e * lax.rsqrt(e) - pt[m * 8 + 6 : m * 8 + 7, :]
                a = 1.0 / (1.0 + d)
                ax = a * pt[m * 8 + 3 : m * 8 + 4, :]
                ay = a * pt[m * 8 + 4 : m * 8 + 5, :]
                az = a * pt[m * 8 + 5 : m * 8 + 6, :]
                if m == 0:
                    near, ws, vx, vy, vz = signed, a, ax, ay, az
                else:
                    near = jnp.minimum(near, signed)
                    ws, vx, vy, vz = ws + a, vx + ax, vy + ay, vz + az
            ind = 0.5 - 0.5 * jnp.tanh(near)
            scale = 1.0 / ws
            pay = jnp.concatenate(
                [ind, ind * (vx * scale), ind * (vy * scale), ind * (vz * scale)], axis=0
            ).astype(BF16)
            summed = nt_dot(pay, block_hot).astype(BF16).astype(F32)
            base = pl.multiple_of(i * slab + lo_row, half)
            for c in range(4):
                ob[c, pl.ds(base, half), :] = summed[c * half : (c + 1) * half, :]
        return 0

    lax.fori_loop(0, BE, build, 0)
    diag[...] = 6.0 + PENALTY * ob[0]
    src[...] = src[...] - ((ob[1] + ob[2]) + ob[3])

    def product(a, b):
        wide = nn_dot(mh[a:b, :], rhs[...])
        return (wide[:, :lanes] + wide[:, lanes:]) + nn_dot(ml[a:b, :], rhs[:, :lanes])

    bz8 = lane8 % bz_n
    bx8 = (lane8 // bz_n) % bx_n
    bx64 = (lane64 // bz_n) % bx_n
    bx32 = (lane32 // bz_n) % bx_n

    def turn(x, shift):
        shift = shift % lanes
        return x if shift == 0 else pltpu.roll(x, shift, axis=1)

    def halo(turn_no):
        def copy(buf, dst, k, device):
            return pltpu.make_async_remote_copy(
                src_ref=buf,
                dst_ref=dst.at[turn_no],
                send_sem=hsend_sem.at[turn_no, k],
                recv_sem=hrecv_sem.at[turn_no, k],
                device_id=device,
                device_id_type=MESH,
            )

        down_c = copy(xsend.at[turn_no, 0], xhigh, 0, (mf, lax.max(mc - 1, 0)))
        up_c = copy(xsend.at[turn_no, 1], xlow, 1, (mf, lax.min(mc + 1, nc - 1)))
        down_f = copy(zsend.at[turn_no, 0], zhigh, 2, (lax.max(mf - 1, 0), mc))
        up_f = copy(zsend.at[turn_no, 1], zlow, 3, (lax.min(mf + 1, nf - 1), mc))
        return down_c, up_c, down_f, up_f

    def apply(value, v_ref, out_ref, turn_no, between=None):
        down_c, up_c, down_f, up_f = halo(turn_no)
        has = (mc > 0, mc < nc - 1, mf > 0, mf < nf - 1)
        vh = value.astype(BF16)
        rhs[:, :lanes] = vh
        rhs[:, lanes:] = (value - vh.astype(F32)).astype(BF16)
        ends = product(0, 2 * slab)
        v0, v7 = ends[:slab], ends[slab:]
        v_ref[0:slab, :] = v0
        v_ref[cells - slab : cells, :] = v7
        xsend[turn_no, 0] = jnp.where(bx32 == 0, v0[:half], turn(v0[half:], bz_n))
        xsend[turn_no, 1] = jnp.where(bx32 == 0, turn(v7[:half], -bz_n), v7[half:])
        for cond, cp in zip(has[:2], (down_c, up_c)):
            pl.when(cond)(cp.start)
        v_ref[slab : cells - slab, :] = product(2 * slab, cells)
        for t in range(2):
            lowp = highp = None
            for a in range(bz_n):
                start = (t * bz_n + a) * slab
                lo = turn(v_ref[start : start + BE, :], a)
                hg = turn(v_ref[start + slab - BE : start + slab, :], a - (bz_n - 1))
                lowp = lo if a == 0 else jnp.where(bz8 == a, lo, lowp)
                highp = hg if a == 0 else jnp.where(bz8 == a, hg, highp)
            zsend[turn_no, 0, t * BE : (t + 1) * BE, :] = lowp
            zsend[turn_no, 1, t * BE : (t + 1) * BE, :] = highp
        for cond, cp in zip(has[2:], (down_f, up_f)):
            pl.when(cond)(cp.start)
        if between is not None:
            between()

        v0 = v_ref[0:slab, :]
        v7 = v_ref[cells - slab : cells, :]
        for i in range(BE):
            v = v_ref[i * slab : (i + 1) * slab, :]
            if i > 0:
                beside = v_ref[(i - 1) * slab : i * slab, :]
            else:
                beside = jnp.where(bx64 > 0, turn(v7, bz_n), 0.0)
            if i < BE - 1:
                beside = beside + v_ref[(i + 1) * slab : (i + 2) * slab, :]
            else:
                beside = beside + jnp.where(bx64 < bx_n - 1, turn(v0, -bz_n), 0.0)
            rows = []
            for k in range(BE):
                t = v[k * BE : (k + 1) * BE, :]
                if k > 0:
                    s = v[(k - 1) * BE : k * BE, :]
                else:
                    s = jnp.where(bz8 > 0, turn(v[slab - BE :, :], 1), 0.0)
                if k < BE - 1:
                    s = s + v[(k + 1) * BE : (k + 2) * BE, :]
                else:
                    s = s + jnp.where(bz8 < bz_n - 1, turn(v[:BE, :], -1), 0.0)
                down = pltpu.roll(t, 1, axis=0)
                edge = jnp.where(lane8 < group, 0.0, turn(down, group))
                s = s + jnp.where(sub8 == 0, edge, down)
                up = pltpu.roll(t, BE - 1, axis=0)
                edge = jnp.where(lane8 >= lanes - group, 0.0, turn(up, -group))
                s = s + jnp.where(sub8 == BE - 1, edge, up)
                rows.append(s)
            beside = beside + jnp.concatenate(rows, axis=0)
            out_ref[i * slab : (i + 1) * slab, :] = (
                diag[i * slab : (i + 1) * slab, :] * v - beside
            )

        for cond, cp in zip((has[1], has[0], has[3], has[2]), (down_c, up_c, down_f, up_f)):
            pl.when(cond)(cp.wait_recv)
        for cond, cp in zip(has, (down_c, up_c, down_f, up_f)):
            pl.when(cond)(cp.wait_send)

        got = xhigh[turn_no]
        for h, part in enumerate((turn(got, bz_n), got)):
            a = cells - slab + h * half
            out_ref[a : a + half, :] = out_ref[a : a + half, :] - jnp.where(
                bx32 == bx_n - 1, part, 0.0
            )
        got = xlow[turn_no]
        for h, part in enumerate((got, turn(got, -bz_n))):
            a = h * half
            out_ref[a : a + half, :] = out_ref[a : a + half, :] - jnp.where(bx32 == 0, part, 0.0)
        for t in range(2):
            gl = zlow[turn_no, t * BE : (t + 1) * BE, :]
            gh = zhigh[turn_no, t * BE : (t + 1) * BE, :]
            for a in range(bz_n):
                start = (t * bz_n + a) * slab
                out_ref[start : start + BE, :] = out_ref[start : start + BE, :] - jnp.where(
                    bz8 == 0, turn(gl, -a), 0.0
                )
                b = start + slab - BE
                out_ref[b : b + BE, :] = out_ref[b : b + BE, :] - jnp.where(
                    bz8 == bz_n - 1, turn(gh, bz_n - 1 - a), 0.0
                )

    def pack(pairs):
        rows = [jnp.sum(a * b, axis=0, keepdims=True) for a, b in pairs]
        rows += [jnp.zeros((1, lanes), F32)] * (8 - len(rows))
        return jnp.concatenate(rows, axis=0)

    def reduction(no):
        fstart, ffinish = peers(
            "fish", rsend.at[no, 0], rfish.at[no], fsend_sem.at[no], frecv_sem.at[no]
        )
        cstart, cfinish = peers(
            "curve", rsend.at[no, 1], rcurve.at[no], csend_sem.at[no], crecv_sem.at[no]
        )

        def first(tile):
            rsend[no, 0] = tile
            rfish[no, mf] = tile
            fstart()

        def second():
            ffinish()
            tile = jnp.sum(rfish[no], axis=0)
            rsend[no, 1] = tile
            rcurve[no, mc] = tile
            cstart()

        def last():
            cfinish()
            tile = jnp.sum(rcurve[no], axis=0)
            total = jnp.sum(tile, axis=1, keepdims=True)
            return [total[r : r + 1, :] for r in range(8)]

        return first, second, last

    apply(src[...], y1, v1, 0)
    apply(v1[...], m1, w1, 1)
    first, second, last = reduction(0)
    r, v, w = src[...], v1[...], w1[...]
    first(pack([(r, r), (r, v), (v, v), (v, w), (w, w), (r, w)]))
    apply(w1[...], n1, u1, 2, second)
    for c in range(4):
        def write(x, plane, c=c):
            obf[c, x] = plane.astype(BF16)

        rows_to_field(
            lambda j, c=c: ob[c, pl.ds(j, slab, stride=BE), :], write, bx_n, bz_n, lane64
        )
    out_copy = pltpu.make_async_copy(obf, obst_ref, obf_sem)
    out_copy.start()
    rr, rv, vv, vw, ww, rw, _, _ = last()
    alpha = rr / rv
    ts = (rv - alpha * vv) - alpha * (rw - alpha * vw)
    tt = (vv - alpha * vw) - alpha * (vw - alpha * ww)
    omega = ts / tt
    rho2 = (rr - alpha * rv) - omega * (rv - alpha * rw)
    beta = rho2 / rr * (alpha / omega)

    both, prod = alpha + omega, alpha * omega
    r = src[...]
    v, w = v1[...], w1[...]
    r2 = r - both * v + prod * w
    q = v - both * w + prod * u1[...]
    v2 = q + beta * (v - omega * w)
    mr2 = y1[...] - both * m1[...] + prod * n1[...]
    y2 = mr2 + beta * (y1[...] - omega * m1[...])
    n1[...] = alpha * y1[...] + omega * (y1[...] - alpha * m1[...])
    y1[...] = y2
    m1[...] = mr2
    w1[...] = r2
    u1[...] = q
    v1[...] = v2
    apply(v2, m2, w2, 3)
    r2, q, v2, w = w1[...], u1[...], v1[...], w2[...]
    first, second, last = reduction(1)
    first(
        pack([(src[...], v2), (q, r2), (q, v2), (w, r2), (w, v2), (q, q), (q, w), (w, w)])
    )
    second()
    sv, qr, qv, wr, wv, qq, qw, ww = last()
    alpha2 = rho2 / sv
    ts = (qr - alpha2 * qv) - alpha2 * (wr - alpha2 * wv)
    tt = (qq - alpha2 * qw) - alpha2 * (qw - alpha2 * ww)
    omega2 = ts / tt
    diag[...] = n1[...] + alpha2 * y1[...] + omega2 * (m1[...] - alpha2 * m2[...])
    press_copy = pltpu.make_async_copy(diag, press_hbm, in_sem.at[0])
    press_copy.start()
    src[...] = (w1[...] - alpha2 * v1[...]) - omega2 * (u1[...] - alpha2 * w2[...])
    resid_copy = pltpu.make_async_copy(src, resid_hbm, in_sem.at[1])
    resid_copy.start()
    out_copy.wait()
    press_copy.wait()
    resid_copy.wait()


def local(right_side, block_inverse, midline, entry_fish, entry_seg, entry_dest, entry_block):
    nf, nc = lax.axis_size("fish"), lax.axis_size("curve")
    count = entry_fish.shape[0]
    cap = max(2, 2 * count // nc)
    cx, cz, ny = right_side.shape
    lanes = (cx // BE) * (cz // BE) * (ny // BE)
    cells = BE**3
    slab = BE * BE
    rows, fishes, npts = midline.shape
    width = fishes * npts
    vmem = pl.BlockSpec(memory_space=pltpu.VMEM)
    big = pltpu.VMEM((cells, lanes), F32)
    dma = pltpu.SemaphoreType.DMA
    anywhere = pl.BlockSpec(memory_space=pl.ANY)
    field = jax.ShapeDtypeStruct((cx, cz, ny), F32)
    fields = jax.ShapeDtypeStruct((4, cx, cz, ny), BF16)
    row_form = jax.ShapeDtypeStruct((cells, lanes), F32)
    solved = pl.pallas_call(
        functools.partial(kernel, nf, nc, cap, npts),
        out_shape=(row_form, row_form, fields),
        in_specs=[anywhere] * 2 + [vmem] * 5,
        out_specs=(anywhere,) * 3,
        scratch_shapes=[
            pltpu.VMEM((cx, cz, ny), F32),
            pltpu.VMEM((cells, cells), F32),
            dma((2,)),
            pltpu.VMEM((4, cx, cz, ny), BF16),
            dma,
            pltpu.VMEM((cells, cells), BF16),
            pltpu.VMEM((cells, cells), BF16),
            pltpu.VMEM((cells, 2 * lanes), BF16),
            pltpu.VMEM((8, lanes), F32),
            pltpu.VMEM((8, width), F32),
            pltpu.VMEM((nc, 8, lanes), F32),
            pltpu.VMEM((SEG * 8, width), F32),
            pltpu.VMEM((SEG * 8, lanes), F32),
            pltpu.VMEM((SEG, slab, lanes), F32),
            pltpu.VMEM((4, cells, lanes), F32),
        ]
        + [big] * 10
        + [
            pltpu.VMEM((4, 2, slab // 2, lanes), F32),
            pltpu.VMEM((4, 2, 2 * BE, lanes), F32),
            pltpu.VMEM((4, slab // 2, lanes), F32),
            pltpu.VMEM((4, slab // 2, lanes), F32),
            pltpu.VMEM((4, 2 * BE, lanes), F32),
            pltpu.VMEM((4, 2 * BE, lanes), F32),
            pltpu.VMEM((2, 2, 8, lanes), F32),
            pltpu.VMEM((2, nf, 8, lanes), F32),
            pltpu.VMEM((2, nc, 8, lanes), F32),
            dma((nc,)),
            dma((nc,)),
            dma((4, 4)),
            dma((4, 4)),
            dma((2, nf)),
            dma((2, nf)),
            dma((2, nc)),
            dma((2, nc)),
        ],
        compiler_params=pltpu.CompilerParams(collective_id=0, has_side_effects=True),
    )(
        right_side,
        block_inverse,
        midline,
        *(e.reshape(1, count) for e in (entry_fish, entry_seg, entry_dest, entry_block)),
    )
    return pl.pallas_call(
        finish,
        out_shape=(field, field, fields),
        in_specs=[anywhere] * 3,
        out_specs=(anywhere,) * 3,
        scratch_shapes=[
            big,
            big,
            pltpu.VMEM((cx, cz, ny), F32),
            pltpu.VMEM((cx, cz, ny), F32),
            pltpu.VMEM((4, cx, cz, ny), BF16),
            dma((6,)),
        ],
    )(*solved)


def solution(mesh):
    return jax.shard_map(
        local,
        mesh=mesh,
        in_specs=(
            P("curve", "fish", None),
            P(),
            P(None, "fish", None),
            P(("fish", "curve")),
            P(("fish", "curve")),
            P(("fish", "curve"), None),
            P(("fish", "curve")),
        ),
        out_specs=(
            P("curve", "fish", None),
            P("curve", "fish", None),
            P(None, "curve", "fish", None),
        ),
        check_vma=False,
    )
```

```python
import functools
import jax
import jax.numpy as jnp
from jax import lax
from jax.experimental import pallas as pl
from jax.experimental.pallas import tpu as pltpu
from jax.sharding import PartitionSpec as P

BE = 8
SEG = 16
PENALTY = 4.0
F32 = jnp.float32
BF16 = jnp.bfloat16
MESH = pl.DeviceIdType.MESH


def nt_dot(a, b):
    return lax.dot_general(a, b, (((1,), (1,)), ((), ())), preferred_element_type=F32)


def nn_dot(a, b):
    return lax.dot_general(a, b, (((1,), (0,)), ((), ())), preferred_element_type=F32)


def split3(x):
    hi = x.astype(BF16)
    rest = x - hi.astype(F32)
    mid = rest.astype(BF16)
    low = (rest - mid.astype(F32)).astype(BF16)
    return hi, mid, low


def swap_bits(arrays, lane):
    arrays = list(arrays)
    lanes = lane.shape[-1]
    for step in (4, 2, 1):
        clear = (lane & step) == 0
        for a in range(8):
            if a & step:
                continue
            low, high = arrays[a], arrays[a | step]
            arrays[a] = jnp.where(clear, low, pltpu.roll(high, step, axis=1))
            arrays[a | step] = jnp.where(clear, pltpu.roll(low, lanes - step, axis=1), high)
    return arrays


def rows_to_field(read_j, write, bx_n, bz_n, lane):
    parts = swap_bits([read_j(j) for j in range(BE)], lane)
    for bx in range(bx_n):
        for i in range(BE):
            plane = jnp.concatenate(
                [parts[bx * bz_n + bz][i * BE : (i + 1) * BE, :] for bz in range(bz_n)], axis=0
            )
            write(bx * BE + i, plane)


def finish(
    prow_ref, rrow_ref, oin_ref, press_ref, resid_ref, obst_ref, prow, rrow, pf, rf, of, sems
):
    slab = BE * BE
    bx_n, bz_n = pf.shape[0] // BE, pf.shape[1] // BE
    lane = lax.broadcasted_iota(jnp.int32, (slab, prow.shape[1]), 1)
    take = [
        pltpu.make_async_copy(a, b, sems.at[n])
        for n, (a, b) in enumerate(((prow_ref, prow), (rrow_ref, rrow), (oin_ref, of)))
    ]
    give = [
        pltpu.make_async_copy(a, b, sems.at[3 + n])
        for n, (a, b) in enumerate(((pf, press_ref), (rf, resid_ref), (of, obst_ref)))
    ]
    for copy in take:
        copy.start()
    for n, (rows, field) in enumerate(((prow, pf), (rrow, rf))):
        take[n].wait()

        def write(x, plane, field=field):
            field[x] = plane

        rows_to_field(
            lambda j, rows=rows: rows[pl.ds(j, slab, stride=BE), :], write, bx_n, bz_n, lane
        )
        give[n].start()
        if n == 0:
            take[2].wait()
            give[2].start()
    for copy in give:
        copy.wait()


def kernel(
    nf, nc, cap, npts,
    rs_hbm, inv_hbm, mid_ref, fish_ref, seg_ref, dest_ref, block_ref,
    press_hbm, resid_hbm, obst_ref,
    rs_ref, inv_ref, in_sem, obf, obf_sem, mh, ml, rhs, meta_ref, tab, gath, shifted, pt, dyz, ob, src, diag,
    y1, v1, m1, w1, n1, u1, m2, w2,
    xsend, zsend, xlow, xhigh, zlow, zhigh, rsend, rfish, rcurve,
    gsend_sem, grecv_sem, hsend_sem, hrecv_sem, fsend_sem, frecv_sem, csend_sem, crecv_sem,
):
    mf = lax.axis_index("fish")
    mc = lax.axis_index("curve")
    cells, lanes = src.shape
    slab = BE * BE
    bx_n = rs_ref.shape[0] // BE
    bz_n = rs_ref.shape[1] // BE
    group = bx_n * bz_n

    inv_copy = pltpu.make_async_copy(inv_hbm, inv_ref, in_sem.at[0])
    rs_copy = pltpu.make_async_copy(rs_hbm, rs_ref, in_sem.at[1])
    inv_copy.start()
    rs_copy.start()

    barrier = pltpu.get_barrier_semaphore()

    def greet_fish(k, _):
        pl.semaphore_signal(
            barrier, inc=1, device_id=(lax.rem(mf + k, nf), mc), device_id_type=MESH
        )
        return 0

    def greet_curve(k, _):
        pl.semaphore_signal(
            barrier, inc=1, device_id=(mf, lax.rem(mc + k, nc)), device_id_type=MESH
        )
        return 0

    nyb = rs_ref.shape[2] // BE
    count = fish_ref.shape[1]
    meta_ref[...] = jnp.full_like(meta_ref, -1.0)
    block = block_ref[...]
    place_in = block % nyb * group + block // nyb + 1
    for r, column in enumerate((fish_ref[...], seg_ref[...], dest_ref[...], place_in)):
        meta_ref[r : r + 1, 0:count] = column.astype(F32)
    xlow[...] = jnp.zeros_like(xlow)
    xhigh[...] = jnp.zeros_like(xhigh)
    zlow[...] = jnp.zeros_like(zlow)
    zhigh[...] = jnp.zeros_like(zhigh)
    lax.fori_loop(1, nf, greet_fish, 0)
    lax.fori_loop(1, nc, greet_curve, 0)

    def peers(axis, src_at, dst, send_sem, recv_sem):
        count = nf if axis == "fish" else nc
        me = mf if axis == "fish" else mc

        def copy(k, slot, target):
            device = (target, mc) if axis == "fish" else (mf, target)
            return pltpu.make_async_remote_copy(
                src_ref=src_at,
                dst_ref=dst.at[slot],
                send_sem=send_sem.at[k],
                recv_sem=recv_sem.at[k],
                device_id=device,
                device_id_type=MESH,
            )

        def start():
            def body(k, _):
                copy(k, me, lax.rem(me + k, count)).start()
                return 0

            lax.fori_loop(1, count, body, 0)

        def finish():
            def body(k, _):
                origin = lax.rem(me + count - k, count)
                copy(k, origin, origin).wait()
                return 0

            lax.fori_loop(1, count, body, 0)

        return start, finish

    pl.semaphore_wait(barrier, nf - 1 + nc - 1)
    gstart, gfinish = peers("curve", meta_ref, gath, gsend_sem, grecv_sem)
    gath[mc] = meta_ref[...]
    gstart()

    lane8 = lax.broadcasted_iota(jnp.int32, (BE, lanes), 1)
    lane64 = lax.broadcasted_iota(jnp.int32, (slab, lanes), 1)
    lane32 = lax.broadcasted_iota(jnp.int32, (slab // 2, lanes), 1)
    sub8 = lax.broadcasted_iota(jnp.int32, (BE, lanes), 0)

    rows, fishes, _ = mid_ref.shape
    width = tab.shape[1]
    for f in range(fishes):
        tab[0:rows, f * npts : (f + 1) * npts] = mid_ref[:, f, :]
    tab[rows:8, :] = jnp.zeros((8 - rows, width), F32)
    table = tab[...]
    for m in range(SEG):
        turned = table if m == 0 else pltpu.roll(table, width - m, axis=1)
        shifted[m * 8 : m * 8 + 8, :] = turned

    inv_copy.wait()
    whole = inv_ref[...]
    hi = whole.astype(BF16)
    low = (whole - hi.astype(F32)).astype(BF16)
    for full, kept in ((hi, mh), (low, ml)):
        kept[0:slab, :] = full[0:slab, :]
        kept[slab : 2 * slab, :] = full[cells - slab :, :]
        kept[2 * slab :, :] = full[slab : cells - slab, :]

    def field_to_rows(read, out_ref):
        parts = []
        for g in range(group):
            bx, bz = g // bz_n, g % bz_n
            parts.append(read(bx, bz).reshape(slab, lanes))
        for j, rows in enumerate(swap_bits(parts, lane64)):
            out_ref[pl.ds(j, slab, stride=BE), :] = rows

    rs_copy.wait()
    field_to_rows(
        lambda bx, bz: rs_ref[bx * BE : (bx + 1) * BE, bz * BE : (bz + 1) * BE, :], src
    )

    gfinish()

    col = lax.broadcasted_iota(jnp.int32, (lanes, lanes), 1)
    row = lax.broadcasted_iota(jnp.int32, (lanes, lanes), 0)
    earlier = jnp.where(row < col, 1.0, 0.0).astype(BF16)
    mine = gath[:, 2, :] == mc.astype(F32)
    rank = nn_dot(jnp.where(mine, 1.0, 0.0).astype(BF16), earlier)
    origin = lax.broadcasted_iota(jnp.int32, (nc, lanes), 0).astype(F32)
    slot = jnp.where(mine, origin * cap + rank, -1.0)
    rowf = row.astype(F32)
    picked = jnp.zeros((8, lanes), F32)
    for c in range(nc):
        hot = jnp.where(rowf == slot[c : c + 1, :], 1.0, 0.0).astype(BF16)
        picked = picked + nt_dot(gath[c].astype(BF16), hot)
    index = picked[0:1, :] * npts + picked[1:2, :]
    place = picked[3:4, :] - 1.0
    block_hot = jnp.where(rowf == place, 1.0, 0.0).astype(BF16)
    point_hot = jnp.where(
        lax.broadcasted_iota(jnp.int32, (width, lanes), 0).astype(F32) == index, 1.0, 0.0
    ).astype(BF16)
    hi, mid, low = split3(shifted[...])
    pt[...] = (nn_dot(hi, point_hot) + nn_dot(mid, point_hot)) + nn_dot(low, point_hot)

    cell = lax.broadcasted_iota(jnp.int32, (slab, lanes), 0)
    zc = (cell // BE).astype(F32) + 0.5
    yc = (cell % BE).astype(F32) + 0.5
    for m in range(SEG):
        dy = yc - pt[m * 8 + 1 : m * 8 + 2, :]
        dz = zc - pt[m * 8 + 2 : m * 8 + 3, :]
        dyz[m] = dy * dy + dz * dz

    half = slab // 2

    def build(i, _):
        xc = i.astype(F32) + 0.5
        for h in range(2):
            lo_row = h * half
            near = ws = vx = vy = vz = None
            for m in range(SEG):
                dx = xc - pt[m * 8 : m * 8 + 1, :]
                d = dyz[m, lo_row : lo_row + half, :] + dx * dx
                e = d + 0.25
                signed = e * lax.rsqrt(e) - pt[m * 8 + 6 : m * 8 + 7, :]
                a = 1.0 / (1.0 + d)
                ax = a * pt[m * 8 + 3 : m * 8 + 4, :]
                ay = a * pt[m * 8 + 4 : m * 8 + 5, :]
                az = a * pt[m * 8 + 5 : m * 8 + 6, :]
                if m == 0:
                    near, ws, vx, vy, vz = signed, a, ax, ay, az
                else:
                    near = jnp.minimum(near, signed)
                    ws, vx, vy, vz = ws + a, vx + ax, vy + ay, vz + az
            ind = 0.5 - 0.5 * jnp.tanh(near)
            scale = 1.0 / ws
            pay = jnp.concatenate(
                [ind, ind * (vx * scale), ind * (vy * scale), ind * (vz * scale)], axis=0
            ).astype(BF16)
            summed = nt_dot(pay, block_hot).astype(BF16).astype(F32)
            base = pl.multiple_of(i * slab + lo_row, half)
            for c in range(4):
                ob[c, pl.ds(base, half), :] = summed[c * half : (c + 1) * half, :]
        return 0

    lax.fori_loop(0, BE, build, 0)
    diag[...] = 6.0 + PENALTY * ob[0]
    src[...] = src[...] - ((ob[1] + ob[2]) + ob[3])

    def product(a, b):
        wide = nn_dot(mh[a:b, :], rhs[...])
        return (wide[:, :lanes] + wide[:, lanes:]) + nn_dot(ml[a:b, :], rhs[:, :lanes])

    bz8 = lane8 % bz_n
    bx8 = (lane8 // bz_n) % bx_n
    bx64 = (lane64 // bz_n) % bx_n
    bx32 = (lane32 // bz_n) % bx_n

    def turn(x, shift):
        shift = shift % lanes
        return x if shift == 0 else pltpu.roll(x, shift, axis=1)

    def halo(turn_no):
        def copy(buf, dst, k, device):
            return pltpu.make_async_remote_copy(
                src_ref=buf,
                dst_ref=dst.at[turn_no],
                send_sem=hsend_sem.at[turn_no, k],
                recv_sem=hrecv_sem.at[turn_no, k],
                device_id=device,
                device_id_type=MESH,
            )

        down_c = copy(xsend.at[turn_no, 0], xhigh, 0, (mf, lax.max(mc - 1, 0)))
        up_c = copy(xsend.at[turn_no, 1], xlow, 1, (mf, lax.min(mc + 1, nc - 1)))
        down_f = copy(zsend.at[turn_no, 0], zhigh, 2, (lax.max(mf - 1, 0), mc))
        up_f = copy(zsend.at[turn_no, 1], zlow, 3, (lax.min(mf + 1, nf - 1), mc))
        return down_c, up_c, down_f, up_f

    def apply(value, v_ref, out_ref, turn_no, between=None):
        down_c, up_c, down_f, up_f = halo(turn_no)
        has = (mc > 0, mc < nc - 1, mf > 0, mf < nf - 1)
        vh = value.astype(BF16)
        rhs[:, :lanes] = vh
        rhs[:, lanes:] = (value - vh.astype(F32)).astype(BF16)
        ends = product(0, 2 * slab)
        v0, v7 = ends[:slab], ends[slab:]
        v_ref[0:slab, :] = v0
        v_ref[cells - slab : cells, :] = v7
        xsend[turn_no, 0] = jnp.where(bx32 == 0, v0[:half], turn(v0[half:], bz_n))
        xsend[turn_no, 1] = jnp.where(bx32 == 0, turn(v7[:half], -bz_n), v7[half:])
        for cond, cp in zip(has[:2], (down_c, up_c)):
            pl.when(cond)(cp.start)
        v_ref[slab : cells - slab, :] = product(2 * slab, cells)
        for t in range(2):
            lowp = highp = None
            for a in range(bz_n):
                start = (t * bz_n + a) * slab
                lo = turn(v_ref[start : start + BE, :], a)
                hg = turn(v_ref[start + slab - BE : start + slab, :], a - (bz_n - 1))
                lowp = lo if a == 0 else jnp.where(bz8 == a, lo, lowp)
                highp = hg if a == 0 else jnp.where(bz8 == a, hg, highp)
            zsend[turn_no, 0, t * BE : (t + 1) * BE, :] = lowp
            zsend[turn_no, 1, t * BE : (t + 1) * BE, :] = highp
        for cond, cp in zip(has[2:], (down_f, up_f)):
            pl.when(cond)(cp.start)
        if between is not None:
            between()

        v0 = v_ref[0:slab, :]
        v7 = v_ref[cells - slab : cells, :]
        for i in range(BE):
            v = v_ref[i * slab : (i + 1) * slab, :]
            if i > 0:
                beside = v_ref[(i - 1) * slab : i * slab, :]
            else:
                beside = jnp.where(bx64 > 0, turn(v7, bz_n), 0.0)
            if i < BE - 1:
                beside = beside + v_ref[(i + 1) * slab : (i + 2) * slab, :]
            else:
                beside = beside + jnp.where(bx64 < bx_n - 1, turn(v0, -bz_n), 0.0)
            rows = []
            for k in range(BE):
                t = v[k * BE : (k + 1) * BE, :]
                if k > 0:
                    s = v[(k - 1) * BE : k * BE, :]
                else:
                    s = jnp.where(bz8 > 0, turn(v[slab - BE :, :], 1), 0.0)
                if k < BE - 1:
                    s = s + v[(k + 1) * BE : (k + 2) * BE, :]
                else:
                    s = s + jnp.where(bz8 < bz_n - 1, turn(v[:BE, :], -1), 0.0)
                down = pltpu.roll(t, 1, axis=0)
                edge = jnp.where(lane8 < group, 0.0, turn(down, group))
                s = s + jnp.where(sub8 == 0, edge, down)
                up = pltpu.roll(t, BE - 1, axis=0)
                edge = jnp.where(lane8 >= lanes - group, 0.0, turn(up, -group))
                s = s + jnp.where(sub8 == BE - 1, edge, up)
                rows.append(s)
            beside = beside + jnp.concatenate(rows, axis=0)
            out_ref[i * slab : (i + 1) * slab, :] = (
                diag[i * slab : (i + 1) * slab, :] * v - beside
            )

        for cond, cp in zip((has[1], has[0], has[3], has[2]), (down_c, up_c, down_f, up_f)):
            pl.when(cond)(cp.wait_recv)

        got = xhigh[turn_no]
        for h, part in enumerate((turn(got, bz_n), got)):
            a = cells - slab + h * half
            out_ref[a : a + half, :] = out_ref[a : a + half, :] - jnp.where(
                bx32 == bx_n - 1, part, 0.0
            )
        got = xlow[turn_no]
        for h, part in enumerate((got, turn(got, -bz_n))):
            a = h * half
            out_ref[a : a + half, :] = out_ref[a : a + half, :] - jnp.where(bx32 == 0, part, 0.0)
        for t in range(2):
            gl = zlow[turn_no, t * BE : (t + 1) * BE, :]
            gh = zhigh[turn_no, t * BE : (t + 1) * BE, :]
            for a in range(bz_n):
                start = (t * bz_n + a) * slab
                out_ref[start : start + BE, :] = out_ref[start : start + BE, :] - jnp.where(
                    bz8 == 0, turn(gl, -a), 0.0
                )
                b = start + slab - BE
                out_ref[b : b + BE, :] = out_ref[b : b + BE, :] - jnp.where(
                    bz8 == bz_n - 1, turn(gh, bz_n - 1 - a), 0.0
                )
        for cond, cp in zip(has, (down_c, up_c, down_f, up_f)):
            pl.when(cond)(cp.wait_send)

    def pack(pairs):
        rows = [jnp.sum(a * b, axis=0, keepdims=True) for a, b in pairs]
        rows += [jnp.zeros((1, lanes), F32)] * (8 - len(rows))
        return jnp.concatenate(rows, axis=0)

    def reduction(no):
        fstart, ffinish = peers(
            "fish", rsend.at[no, 0], rfish.at[no], fsend_sem.at[no], frecv_sem.at[no]
        )
        cstart, cfinish = peers(
            "curve", rsend.at[no, 1], rcurve.at[no], csend_sem.at[no], crecv_sem.at[no]
        )

        def first(tile):
            rsend[no, 0] = tile
            rfish[no, mf] = tile
            fstart()

        def second():
            ffinish()
            tile = jnp.sum(rfish[no], axis=0)
            rsend[no, 1] = tile
            rcurve[no, mc] = tile
            cstart()

        def last():
            cfinish()
            tile = jnp.sum(rcurve[no], axis=0)
            total = jnp.sum(tile, axis=1, keepdims=True)
            return [total[r : r + 1, :] for r in range(8)]

        return first, second, last

    apply(src[...], y1, v1, 0)
    apply(v1[...], m1, w1, 1)
    first, second, last = reduction(0)
    r, v, w = src[...], v1[...], w1[...]
    first(pack([(r, r), (r, v), (v, v), (v, w), (w, w), (r, w)]))
    apply(w1[...], n1, u1, 2, second)
    for c in range(4):
        def write(x, plane, c=c):
            obf[c, x] = plane.astype(BF16)

        rows_to_field(
            lambda j, c=c: ob[c, pl.ds(j, slab, stride=BE), :], write, bx_n, bz_n, lane64
        )
    out_copy = pltpu.make_async_copy(obf, obst_ref, obf_sem)
    out_copy.start()
    rr, rv, vv, vw, ww, rw, _, _ = last()
    alpha = rr / rv
    ts = (rv - alpha * vv) - alpha * (rw - alpha * vw)
    tt = (vv - alpha * vw) - alpha * (vw - alpha * ww)
    omega = ts / tt
    rho2 = (rr - alpha * rv) - omega * (rv - alpha * rw)
    beta = rho2 / rr * (alpha / omega)

    both, prod = alpha + omega, alpha * omega
    r = src[...]
    v, w = v1[...], w1[...]
    r2 = r - both * v + prod * w
    q = v - both * w + prod * u1[...]
    v2 = q + beta * (v - omega * w)
    mr2 = y1[...] - both * m1[...] + prod * n1[...]
    y2 = mr2 + beta * (y1[...] - omega * m1[...])
    n1[...] = alpha * y1[...] + omega * (y1[...] - alpha * m1[...])
    y1[...] = y2
    m1[...] = mr2
    w1[...] = r2
    u1[...] = q
    v1[...] = v2
    apply(v2, m2, w2, 3)
    r2, q, v2, w = w1[...], u1[...], v1[...], w2[...]
    first, second, last = reduction(1)
    first(
        pack([(src[...], v2), (q, r2), (q, v2), (w, r2), (w, v2), (q, q), (q, w), (w, w)])
    )
    second()
    sv, qr, qv, wr, wv, qq, qw, ww = last()
    alpha2 = rho2 / sv
    ts = (qr - alpha2 * qv) - alpha2 * (wr - alpha2 * wv)
    tt = (qq - alpha2 * qw) - alpha2 * (qw - alpha2 * ww)
    omega2 = ts / tt
    diag[...] = n1[...] + alpha2 * y1[...] + omega2 * (m1[...] - alpha2 * m2[...])
    press_copy = pltpu.make_async_copy(diag, press_hbm, in_sem.at[0])
    press_copy.start()
    src[...] = (w1[...] - alpha2 * v1[...]) - omega2 * (u1[...] - alpha2 * w2[...])
    resid_copy = pltpu.make_async_copy(src, resid_hbm, in_sem.at[1])
    resid_copy.start()
    out_copy.wait()
    press_copy.wait()
    resid_copy.wait()


def local(right_side, block_inverse, midline, entry_fish, entry_seg, entry_dest, entry_block):
    nf, nc = lax.axis_size("fish"), lax.axis_size("curve")
    count = entry_fish.shape[0]
    cap = max(2, 2 * count // nc)
    cx, cz, ny = right_side.shape
    lanes = (cx // BE) * (cz // BE) * (ny // BE)
    cells = BE**3
    slab = BE * BE
    rows, fishes, npts = midline.shape
    width = fishes * npts
    vmem = pl.BlockSpec(memory_space=pltpu.VMEM)
    big = pltpu.VMEM((cells, lanes), F32)
    dma = pltpu.SemaphoreType.DMA
    anywhere = pl.BlockSpec(memory_space=pl.ANY)
    field = jax.ShapeDtypeStruct((cx, cz, ny), F32)
    fields = jax.ShapeDtypeStruct((4, cx, cz, ny), BF16)
    row_form = jax.ShapeDtypeStruct((cells, lanes), F32)
    solved = pl.pallas_call(
        functools.partial(kernel, nf, nc, cap, npts),
        out_shape=(row_form, row_form, fields),
        in_specs=[anywhere] * 2 + [vmem] * 5,
        out_specs=(anywhere,) * 3,
        scratch_shapes=[
            pltpu.VMEM((cx, cz, ny), F32),
            pltpu.VMEM((cells, cells), F32),
            dma((2,)),
            pltpu.VMEM((4, cx, cz, ny), BF16),
            dma,
            pltpu.VMEM((cells, cells), BF16),
            pltpu.VMEM((cells, cells), BF16),
            pltpu.VMEM((cells, 2 * lanes), BF16),
            pltpu.VMEM((8, lanes), F32),
            pltpu.VMEM((8, width), F32),
            pltpu.VMEM((nc, 8, lanes), F32),
            pltpu.VMEM((SEG * 8, width), F32),
            pltpu.VMEM((SEG * 8, lanes), F32),
            pltpu.VMEM((SEG, slab, lanes), F32),
            pltpu.VMEM((4, cells, lanes), F32),
        ]
        + [big] * 10
        + [
            pltpu.VMEM((4, 2, slab // 2, lanes), F32),
            pltpu.VMEM((4, 2, 2 * BE, lanes), F32),
            pltpu.VMEM((4, slab // 2, lanes), F32),
            pltpu.VMEM((4, slab // 2, lanes), F32),
            pltpu.VMEM((4, 2 * BE, lanes), F32),
            pltpu.VMEM((4, 2 * BE, lanes), F32),
            pltpu.VMEM((2, 2, 8, lanes), F32),
            pltpu.VMEM((2, nf, 8, lanes), F32),
            pltpu.VMEM((2, nc, 8, lanes), F32),
            dma((nc,)),
            dma((nc,)),
            dma((4, 4)),
            dma((4, 4)),
            dma((2, nf)),
            dma((2, nf)),
            dma((2, nc)),
            dma((2, nc)),
        ],
        compiler_params=pltpu.CompilerParams(collective_id=0, has_side_effects=True),
    )(
        right_side,
        block_inverse,
        midline,
        *(e.reshape(1, count) for e in (entry_fish, entry_seg, entry_dest, entry_block)),
    )
    return pl.pallas_call(
        finish,
        out_shape=(field, field, fields),
        in_specs=[anywhere] * 3,
        out_specs=(anywhere,) * 3,
        scratch_shapes=[
            big,
            big,
            pltpu.VMEM((cx, cz, ny), F32),
            pltpu.VMEM((cx, cz, ny), F32),
            pltpu.VMEM((4, cx, cz, ny), BF16),
            dma((6,)),
        ],
    )(*solved)


def solution(mesh):
    return jax.shard_map(
        local,
        mesh=mesh,
        in_specs=(
            P("curve", "fish", None),
            P(),
            P(None, "fish", None),
            P(("fish", "curve")),
            P(("fish", "curve")),
            P(("fish", "curve"), None),
            P(("fish", "curve")),
        ),
        out_specs=(
            P("curve", "fish", None),
            P("curve", "fish", None),
            P(None, "curve", "fish", None),
        ),
        check_vma=False,
    )
```
